128 devices in a mesh: arrow: 4 (over z_lo, core), blk: 32 (over x, y, z_hi).
Axes of the slice: x: 4, y: 4, z: 4 (z_hi: 2, z_lo: 2; z = z_hi * 2 + z_lo), core: 2. Of those that a mesh axis runs over, the one named last changes fastest.
Arguments:
- features: bfloat16 [32768, 512], P(('arrow', 'blk')), may hold values from -6 to 6
- positions: int32 [4, 32768], P(None, ('arrow', 'blk')), may hold values from 0 to 32767, as said below
- diag_values: bfloat16 [4096, 32768], P('arrow', 'blk'), may hold values from -0.1875 to 0.1875
- column_values: bfloat16 [4096, 32768], P('arrow', 'blk'), may hold values from -0.1875 to 0.1875
- row_values: bfloat16 [4096, 32768], P('arrow', 'blk'), may hold values from -0.03125 to 0.03125
- tile_masks: int32 [3, 32, 256], P(None, 'arrow', 'blk'), may hold values from 0 to 1, as said below
- up_weight: bfloat16 [1024, 4096], replicated, may hold values from -0.1875 to 0.1875
- down_weight: bfloat16 [4096, 512], replicated, may hold values from -0.09375 to 0.09375
Outputs:
- node_out: bfloat16 [32768, 512], P(('arrow', 'blk'))
The draws below stay inside these ranges and needn't reach their ends.
Inputs may be any that keep to these rules, and one draw needn't show every extreme that they name: For each arrow, positions is a permutation of the nodes. The 256 nodes of one device put at most 12 nodes into any one block of 1024 positions of one arrow, and exactly 12 into some block. `tile_masks`: 1 marks a stored tile, 0 an empty one.
All inputs are finite; a program needn't handle non-finite values.
Results may differ from the reference program's by a relative error of at most 0.0085.
Values may be sent and summed in bfloat16 or wider, within the bound.
No kernel may reach another device: no remote copies, remote signals or barrier semaphores. Data moves between devices by JAX's collectives and lax.ppermute only.
A program may use at most 64 MiB of HBM per device.

```python
import jax
import jax.numpy as jnp
from jax import lax

F = 512
FF = 4096
R = 256
BS = 1024
NT = 8
NODES = 32768
N_ARROW = 4
N_BLK = 32


def draw_positions(key, part):
    block_count = NODES // BS
    arrow_count = BS // R
    device_count = arrow_count * block_count
    base_count = R // block_count
    half_spread = max(R // (2 * block_count), 1)
    source = jnp.arange(device_count, dtype=jnp.int32)
    column = jnp.arange(block_count, dtype=jnp.int32)
    rank_ids = jnp.arange(R, dtype=jnp.int32)

    def one_arrow(arrow_key):
        sub_keys = jax.random.split(arrow_key, 4)
        spread = jax.random.randint(sub_keys[0], (block_count // 2,), -half_spread, half_spread + 1, dtype=jnp.int32)
        spread = spread.at[0].set(half_spread)
        shifts = jax.random.permutation(sub_keys[1], jnp.concatenate([spread, -spread])).astype(jnp.int32)
        counts = base_count + shifts[(column[None, :] - source[:, None]) % block_count]
        upper_cum = jnp.cumsum(counts, axis=1)
        lower_cum = upper_cum - counts
        target = jnp.sum((upper_cum[:, None, :] <= rank_ids[None, :, None]).astype(jnp.int32), axis=2)
        inner_rank = rank_ids[None, :] - jnp.take_along_axis(lower_cum, target, axis=1)
        offset = jnp.cumsum(counts, axis=0) - counts
        slot_pos = jnp.take_along_axis(offset, target, axis=1) + inner_rank
        orders = jax.vmap(lambda sub_key: jax.random.permutation(sub_key, R).astype(jnp.int32))(jax.random.split(sub_keys[2], device_count))
        shuffles = jax.vmap(lambda sub_key: jax.random.permutation(sub_key, BS).astype(jnp.int32))(jax.random.split(sub_keys[3], block_count))
        final_pos = target * BS + shuffles[target, slot_pos]
        node_ids = source[:, None] * R + orders
        return jnp.zeros((NODES,), jnp.int32).at[node_ids.reshape(-1)].set(final_pos.reshape(-1))
    return jax.vmap(one_arrow)(jax.random.split(jax.random.fold_in(key, 11), arrow_count))


def draw_tile_masks(key, part):
    block_count = NODES // BS
    arrow_count = BS // R
    sub_keys = jax.random.split(jax.random.fold_in(key, 23), 2)
    density = jax.random.randint(sub_keys[0], (3, arrow_count, 1, block_count, 1), 1, 5, dtype=jnp.int32)
    coin_flips = jax.random.randint(sub_keys[1], (3, arrow_count, NT, block_count, NT), 0, 4, dtype=jnp.int32)
    return (coin_flips < density).astype(jnp.int32).reshape(3, arrow_count * NT, block_count * NT)


def levels(key, dims, cuts, smallest, top_value):
    gain, own = 1.0, jax.random.fold_in(key, 6)
    for axis_at, blocks in cuts:
        steps = jnp.exp(jax.random.uniform(jax.random.fold_in(own, axis_at), (blocks,), jnp.float32, smallest / len(cuts), top_value / len(cuts)))
        gain = gain * jnp.repeat(steps, dims[axis_at] // blocks).reshape([-1 if axis == axis_at else 1 for axis in range(len(dims))])
    return gain


def noise(own_key, shape, scale, bound, shards=(), kind=jnp.bfloat16):
    factor_of = levels(own_key, shape, shards, -0.22, 0.18) if shards else 1.0
    result = jax.random.normal(own_key, shape, jnp.float32) * scale * factor_of
    return jnp.minimum(jnp.maximum(result, -bound), bound).astype(kind)


def setup_inputs(seed: int = 0) -> dict:
    key_list = jax.random.split(jax.random.key(seed), 9)
    features = noise(key_list[0], (NODES, F), 1.0, 6.0, ((0, 128),))
    positions = draw_positions(jax.random.fold_in(key_list[8], 71), 0)
    diag_values = noise(key_list[2], (N_ARROW * BS, N_BLK * BS), BS ** -0.5, 0.1875, ((0, 4), (1, 32)))
    column_values = noise(key_list[3], (N_ARROW * BS, N_BLK * BS), BS ** -0.5, 0.1875, ((0, 4), (1, 32)))
    row_values = noise(key_list[4], (N_ARROW * BS, N_BLK * BS), NODES ** -0.5, 0.03125, ((0, 4), (1, 32)))
    tile_masks = draw_tile_masks(jax.random.fold_in(key_list[8], 71), 0)
    up_weight = noise(key_list[6], (2 * F, FF), (2 * F) ** -0.5, 0.1875)
    down_weight = noise(key_list[7], (FF, F), FF ** -0.5, 0.09375)
    return {"features": features, "positions": positions, "diag_values": diag_values, "column_values": column_values, "row_values": row_values, "tile_masks": tile_masks, "up_weight": up_weight, "down_weight": down_weight}


def masked_block(values, tiles):
    tile_count = tiles.shape[0]
    tile_edge = values.shape[0] // tile_count
    shaped = values.reshape(tile_count, tile_edge, tile_count, tile_edge)
    keep_mask = tiles.astype(values.dtype)[:, None, :, None]
    return (shaped * keep_mask).reshape(values.shape)


def reference(features, positions, diag_values, column_values, row_values, tile_masks, up_weight, down_weight):
    feat_width = features.shape[1]
    block_count = NODES // BS
    arrow_count = BS // R
    total = jnp.zeros((NODES, feat_width), jnp.float32)
    for arrow_id in range(arrow_count):
        ordered = jnp.zeros_like(features).at[positions[arrow_id]].set(features)
        block_feats = ordered.reshape(block_count, BS, feat_width)
        head_block = block_feats[0]

        def split_blocks(values):
            return values[arrow_id * BS:(arrow_id + 1) * BS].reshape(BS, block_count, BS).transpose(1, 0, 2)

        def split_masks(kind):
            return tile_masks[kind, arrow_id * NT:(arrow_id + 1) * NT].reshape(NT, block_count, NT).transpose(1, 0, 2)

        stacked = (split_blocks(diag_values), split_blocks(column_values), split_blocks(row_values),
                   split_masks(0), split_masks(1), split_masks(2), block_feats)

        def one_block(items):
            diag_part, column_part, row_part, diag_mask, column_mask, row_mask, local_feats = items
            local_sum = jnp.dot(masked_block(diag_part, diag_mask), local_feats, preferred_element_type=jnp.float32)
            local_sum = local_sum + jnp.dot(masked_block(column_part, column_mask), head_block, preferred_element_type=jnp.float32)
            arm_term = jnp.dot(masked_block(row_part, row_mask), local_feats, preferred_element_type=jnp.float32)
            return local_sum, arm_term

        local_sums, arm_terms = lax.map(one_block, stacked)
        arm_total = jnp.sum(arm_terms, axis=0)
        results = local_sums.at[0].add(arm_total).astype(jnp.bfloat16).reshape(NODES, feat_width)
        total = total + results[positions[arrow_id]].astype(jnp.float32)
    aggregate = total.astype(jnp.bfloat16)
    joined = jnp.concatenate([features, aggregate], axis=1)
    hidden = jax.nn.silu(jnp.dot(joined, up_weight, preferred_element_type=jnp.float32)).astype(jnp.bfloat16)
    return jnp.dot(hidden, down_weight, preferred_element_type=jnp.float32).astype(jnp.bfloat16)
```

```python
import jax
import jax.numpy as jnp
from jax import lax
from jax.sharding import PartitionSpec as P

BF = jnp.bfloat16
F32 = jnp.float32


def exchange(block):
    return lax.all_to_all(block, ("arrow", "blk"), split_axis=0, concat_axis=0, tiled=True)


def masked_block(values, tiles):
    tile_count = tiles.shape[0]
    tile_edge = values.shape[0] // tile_count
    shaped = values.reshape(tile_count, tile_edge, tile_count, tile_edge)
    keep_mask = tiles.astype(values.dtype)[:, None, :, None]
    return (shaped * keep_mask).reshape(values.shape)


def body(
    features, positions, diag_values, column_values, row_values, tile_masks, up_weight, down_weight
):
    row_count, width = features.shape
    arrows = positions.shape[0]
    blocks = lax.axis_size("blk")
    devices = arrows * blocks
    block_rows = diag_values.shape[0]
    rows = devices * 8

    block_of = positions // block_rows
    within = positions % block_rows
    member = block_of[:, None, :] == jnp.arange(blocks, dtype=jnp.int32)[None, :, None]
    member = member.reshape(devices, row_count)
    node = jnp.arange(row_count, dtype=jnp.int32)
    before = (node[:, None] < node[None, :]).astype(BF)
    rank = jnp.dot(member.astype(BF), before, preferred_element_type=F32)
    rank = jnp.where(member, rank, -1.0)
    head_rank = rank.reshape(arrows, blocks, row_count)[:, :1, :]
    head_rank = jnp.broadcast_to(head_rank, (arrows, blocks, row_count)).reshape(rank.shape)
    r = jnp.arange(8, dtype=jnp.int32)[None, :, None]
    rank, head_rank = rank[:, None, :], head_rank[:, None, :]
    rf = r.astype(F32)
    picks = [
        rank == rf,
        jnp.where(r < 4, rank, head_rank) == jnp.where(r < 4, rf + 8, rf + 4),
        head_rank == rf,
    ]
    picks = [p.astype(BF).reshape(rows, row_count) for p in picks]

    coded = jnp.stack([within // 32 + 1, within % 32], axis=-1).astype(BF)
    sent = [jnp.dot(p, features, preferred_element_type=F32).astype(BF) for p in picks]
    places = []
    for p in picks:
        part = p.reshape(arrows, rows // arrows, row_count)
        place = jnp.einsum("amn,anc->amc", part, coded, preferred_element_type=F32)
        places.append(place.reshape(rows, 2))
    places = jnp.concatenate(places, axis=1).astype(BF)
    places = jnp.pad(places, ((0, 0), (0, 128 - places.shape[1])))
    message = jnp.concatenate(sent + [places], axis=1).reshape(devices, 8, 3 * width + 128)
    got = exchange(message).reshape(rows, 3 * width + 128)

    got_rows = [got[:, q * width : (q + 1) * width] for q in range(3)]
    codes = got[:, 3 * width :].astype(F32)
    slot_pos = [
        ((codes[:, 2 * q] - 1.0) * 32.0 + codes[:, 2 * q + 1]).astype(jnp.int32) for q in range(3)
    ]
    is_main = (jnp.arange(rows, dtype=jnp.int32) % 8) < 4
    spots = [
        slot_pos[0],
        jnp.where(is_main, slot_pos[1], -1),
        jnp.where(is_main, -1, slot_pos[1]),
        slot_pos[2],
    ]
    place_ids = jnp.arange(block_rows, dtype=jnp.int32)
    puts = [(place_ids[:, None] == s[None, :]).astype(BF) for s in spots]
    takes = [(s[:, None] == place_ids[None, :]).astype(BF) for s in spots]

    def mm(a, b):
        return jnp.dot(a, b, preferred_element_type=F32)

    block_feats = (mm(puts[0], got_rows[0]) + mm(puts[1], got_rows[1])).astype(BF)
    head_feats = (mm(puts[2], got_rows[1]) + mm(puts[3], got_rows[2])).astype(BF)
    diag_full = masked_block(diag_values, tile_masks[0])
    column_full = masked_block(column_values, tile_masks[1])
    row_full = masked_block(row_values, tile_masks[2])
    arm_term = mm(row_full, block_feats).astype(BF)
    local = (mm(diag_full, block_feats) + mm(column_full, head_feats)).astype(BF)
    back = [
        mm(takes[0], local).astype(BF),
        (mm(takes[1], local) + mm(takes[2], arm_term)).astype(BF),
        mm(takes[3], arm_term).astype(BF),
    ]
    reply = jnp.concatenate(back, axis=1).reshape(devices, 8, 3 * width)
    reply = exchange(reply).reshape(rows, 3 * width)

    aggregate = 0.0
    for q in range(3):
        aggregate = aggregate + lax.dot_general(
            picks[q],
            reply[:, q * width : (q + 1) * width],
            (((0,), (0,)), ((), ())),
            preferred_element_type=F32,
        )
    aggregate = aggregate.astype(BF)
    joined = jnp.concatenate([features, aggregate], axis=1)
    hidden = jax.nn.silu(mm(joined, up_weight)).astype(BF)
    return mm(hidden, down_weight).astype(BF)


def solution(mesh):
    in_specs = (
        P(("arrow", "blk"), None),
        P(None, ("arrow", "blk")),
        P("arrow", "blk"),
        P("arrow", "blk"),
        P("arrow", "blk"),
        P(None, "arrow", "blk"),
        P(),
        P(),
    )
    out_specs = P(("arrow", "blk"), None)
    return jax.shard_map(body, mesh=mesh, in_specs=in_specs, out_specs=out_specs, check_vma=False)
```

```python
import functools

import jax
import jax.numpy as jnp
from jax import lax
from jax.experimental import pallas as pl
from jax.experimental.pallas import tpu as pltpu
from jax.sharding import PartitionSpec as P

BF = jnp.bfloat16
F32 = jnp.float32
VM = pl.BlockSpec(memory_space=pltpu.VMEM)
HB = pl.BlockSpec(memory_space=pltpu.HBM)
MIB = 1 << 20


def exchange(block):
    return lax.all_to_all(block, ("arrow", "blk"), split_axis=0, concat_axis=0, tiled=True)


def mm(a, b):
    return jnp.dot(a, b, preferred_element_type=F32)


def mm_nt(a, b):
    return lax.dot_general(a, b, (((1,), (1,)), ((), ())), preferred_element_type=F32)


def in_hbm(x):
    return pltpu.with_memory_space_constraint(x, pltpu.HBM)


def onehot(mask):
    return jnp.where(mask, 1.0, 0.0).astype(BF)


def slot_targets(r):
    return jnp.where(r < 4, r + 8, r + 4).astype(F32)


def pack_kernel(block_rows, width, feat_ref, pos_ref, out_ref):
    nodes = feat_ref.shape[0]
    rows = out_ref.shape[0]
    feats = feat_ref[...]
    n0 = lax.broadcasted_iota(jnp.int32, (nodes, nodes), 0)
    n1 = lax.broadcasted_iota(jnp.int32, (nodes, nodes), 1)
    before = onehot(n0 < n1)
    slot = lax.broadcasted_iota(jnp.int32, (rows, nodes), 0)
    r = slot % 8
    rf = r.astype(F32)
    code_row = lax.broadcasted_iota(jnp.int32, (128, nodes), 0)
    pos = pos_ref[pl.ds(pl.program_id(0), 1), :]
    within = pos % block_rows
    member = pos // block_rows == slot // 8
    rank = jnp.where(member, mm(onehot(member), before), -1.0)
    head = jnp.broadcast_to(rank[0:1, :], rank.shape)
    picks = (
        onehot(rank == rf),
        onehot(jnp.where(r < 4, rank, head) == slot_targets(r)),
        onehot(head == rf),
    )
    high = (within // 32 + 1).astype(F32)
    low = (within % 32).astype(F32)
    codes = jnp.zeros((rows, 128), F32)
    for q in range(3):
        out_ref[:, q * width : (q + 1) * width] = mm(picks[q], feats).astype(BF)
        table = jnp.where(code_row == 2 * q, high, jnp.where(code_row == 2 * q + 1, low, 0.0))
        codes = codes + mm_nt(picks[q], table.astype(BF))
    out_ref[:, 3 * width :] = codes.astype(BF)


def gather_kernel(arrows, block_rows, pos_ref, out_ref):
    nodes = out_ref.shape[0]
    total = out_ref.shape[1] // 3
    rows = total // arrows
    n0 = lax.broadcasted_iota(jnp.int32, (nodes, nodes), 0)
    n1 = lax.broadcasted_iota(jnp.int32, (nodes, nodes), 1)
    before = onehot(n1 < n0)
    slot = lax.broadcasted_iota(jnp.int32, (nodes, rows), 1)
    block = slot // 8
    r = slot % 8
    rf = r.astype(F32)
    goal = slot_targets(r)
    for a in range(arrows):
        member = pos_ref[:, a : a + 1] // block_rows == block
        rank = jnp.where(member, mm(before, onehot(member)), -1.0)
        head = jnp.broadcast_to(rank[:, 0:1], rank.shape)
        picks = (
            onehot(rank == rf),
            onehot(jnp.where(r < 4, rank, head) == goal),
            onehot(head == rf),
        )
        for q in range(3):
            base = q * total + a * rows
            out_ref[:, base : base + rows] = picks[q]


def middle_kernel(
    width, got_ref, mask_ref, diag_hbm, col_hbm, row_hbm, out_hbm,
    w_ref, x_ref, x0_ref, y_ref, t_ref, p_ref, pt_ref, out_ref, w_sem, out_sem,
):
    slots = got_ref.shape[0]
    size = x_ref.shape[0]
    step = 256
    loads = [
        pltpu.make_async_copy(src, w_ref.at[k], w_sem.at[k])
        for k, src in enumerate((diag_hbm, col_hbm, row_hbm))
    ]
    for copy in loads:
        copy.start()
    codes = got_ref[:, 3 * width :].astype(F32)
    place = (codes - 1.0) * 32.0 + pltpu.roll(codes, 127, 1)
    p_ref[...] = place
    pt_ref[...] = place.T
    lane = lax.broadcasted_iota(jnp.int32, (1, slots), 1) % 8 < 4
    sub = lax.broadcasted_iota(jnp.int32, (step, 1), 0) % 8 < 4

    def unpack(c, carry):
        ids = (lax.broadcasted_iota(jnp.int32, (step, slots), 0) + c * step).astype(F32)
        mid = pt_ref[2:3, :]
        a0 = onehot(pt_ref[0:1, :] == ids)
        a1 = onehot(jnp.where(lane, mid, -1.0) == ids)
        b1 = onehot(jnp.where(lane, -1.0, mid) == ids)
        b2 = onehot(pt_ref[4:5, :] == ids)
        g0 = got_ref[:, 0:width]
        g1 = got_ref[:, width : 2 * width]
        g2 = got_ref[:, 2 * width : 3 * width]
        span = pl.ds(pl.multiple_of(c * step, step), step)
        x_ref[span, :] = (mm(a0, g0) + mm(a1, g1)).astype(BF)
        x0_ref[span, :] = (mm(b1, g1) + mm(b2, g2)).astype(BF)
        return carry

    lax.fori_loop(0, size // step, unpack, 0)
    for copy in loads:
        copy.wait()
    tiles = mask_ref.shape[0] // 3
    edge = size // tiles

    def multiply(c, carry):
        span = pl.ds(pl.multiple_of(c * edge, edge), edge)
        kept = []
        for k in range(3):
            keep = jnp.broadcast_to(mask_ref[pl.ds(k * tiles + c, 1), :], (edge, size))
            kept.append(w_ref[k, span, :] * keep.astype(BF))
        x = x_ref[...]
        t_ref[span, :] = mm(kept[2], x).astype(BF)
        y_ref[span, :] = (mm(kept[0], x) + mm(kept[1], x0_ref[...])).astype(BF)
        return carry

    lax.fori_loop(0, tiles, multiply, 0)

    def store(c):
        span = pl.ds(pl.multiple_of(c * step, step), step)
        return pltpu.make_async_copy(out_ref.at[span, :], out_hbm.at[span, :], out_sem.at[c])

    def pack(c, carry):
        span = pl.ds(pl.multiple_of(c * step, step), step)
        ids = lax.broadcasted_iota(jnp.int32, (step, size), 1).astype(F32)
        mid = p_ref[span, 2:3]
        a0 = onehot(p_ref[span, 0:1] == ids)
        a1 = onehot(jnp.where(sub, mid, -1.0) == ids)
        b1 = onehot(jnp.where(sub, -1.0, mid) == ids)
        b2 = onehot(p_ref[span, 4:5] == ids)
        y = y_ref[...]
        t = t_ref[...]
        out_ref[span, 0:width] = mm(a0, y).astype(BF)
        out_ref[span, width : 2 * width] = (mm(a1, y) + mm(b1, t)).astype(BF)
        out_ref[span, 2 * width : 3 * width] = mm(b2, t).astype(BF)
        store(c).start()
        return carry

    lax.fori_loop(0, slots // step, pack, 0)
    for c in range(slots // step):
        store(c).wait()


CHUNK = 512


def tail_kernel(
    width, reply_ref, pick_hbm, pre_hbm, up_hbm, down_hbm, out_ref,
    pick_ref, pre_ref, up_ref, down_ref, agg_ref, acc_ref, pick_sem, sem,
):
    slots = reply_ref.shape[0]
    count = down_ref.shape[0] // CHUNK

    def loads(c):
        span = pl.ds(pl.multiple_of(c * CHUNK, CHUNK), CHUNK)
        return (
            pltpu.make_async_copy(up_hbm.at[width:, span], up_ref.at[:, span], sem.at[0, c]),
            pltpu.make_async_copy(pre_hbm.at[:, span], pre_ref.at[:, span], sem.at[1, c]),
            pltpu.make_async_copy(down_hbm.at[span, :], down_ref.at[span, :], sem.at[2, c]),
        )

    first = pltpu.make_async_copy(pick_hbm, pick_ref, pick_sem)
    first.start()
    for c in range(count):
        for copy in loads(c):
            copy.start()
    first.wait()
    total = jnp.zeros(agg_ref.shape, F32)
    for q in range(3):
        total = total + mm(
            pick_ref[:, q * slots : (q + 1) * slots], reply_ref[:, q * width : (q + 1) * width]
        )
    agg_ref[...] = total.astype(BF)
    acc_ref[...] = jnp.zeros(acc_ref.shape, F32)

    def chunk(c, carry):
        span = pl.ds(pl.multiple_of(c * CHUNK, CHUNK), CHUNK)
        for copy in loads(c):
            copy.wait()
        v = pre_ref[:, span] + mm(agg_ref[...], up_ref[:, span])
        hidden = (v / (1.0 + jnp.exp(-v))).astype(BF)
        acc_ref[...] += mm(hidden, down_ref[span, :])
        return carry

    lax.fori_loop(0, count, chunk, 0)
    out_ref[...] = acc_ref[...].astype(BF)


def body(
    features, positions, diag_values, column_values, row_values, tile_masks, up_weight, down_weight
):
    row_count, width = features.shape
    arrows = positions.shape[0]
    devices = arrows * lax.axis_size("blk")
    size = diag_values.shape[0]
    hidden = down_weight.shape[0]
    tiles = tile_masks.shape[1]
    rows = devices * 8
    longest = 3 * width + 128

    message = pl.pallas_call(
        functools.partial(pack_kernel, size, width),
        grid=(arrows,),
        in_specs=[
            pl.BlockSpec(features.shape, lambda a: (0, 0)),
            pl.BlockSpec(positions.shape, lambda a: (0, 0)),
        ],
        out_specs=pl.BlockSpec((rows // arrows, longest), lambda a: (a, 0)),
        out_shape=pltpu.HBM((rows, longest), BF),
        compiler_params=pltpu.CompilerParams(vmem_limit_bytes=16 * MIB),
        name="pack",
    )(features, positions)
    got = exchange(message.reshape(devices, 8, longest)).reshape(rows, longest)

    gather = pl.pallas_call(
        functools.partial(gather_kernel, arrows, size),
        in_specs=[VM],
        out_specs=VM,
        out_shape=jax.ShapeDtypeStruct((row_count, 3 * rows), BF),
        compiler_params=pltpu.CompilerParams(vmem_limit_bytes=16 * MIB),
        name="gather",
    )(positions.T)
    pre = mm(features, up_weight[:width])
    keep = jnp.repeat(tile_masks.astype(F32), size // tiles, axis=2).reshape(3 * tiles, size)

    reply = pl.pallas_call(
        functools.partial(middle_kernel, width),
        in_specs=[VM, VM, HB, HB, HB],
        out_specs=HB,
        out_shape=pltpu.HBM((rows, 3 * width), BF),
        scratch_shapes=[pltpu.VMEM((3, size, size), BF)]
        + [pltpu.VMEM((size, width), BF)] * 4
        + [
            pltpu.VMEM((rows, 128), F32),
            pltpu.VMEM((128, rows), F32),
            pltpu.VMEM((rows, 3 * width), BF),
            pltpu.SemaphoreType.DMA((3,)),
            pltpu.SemaphoreType.DMA((rows // 256,)),
        ],
        compiler_params=pltpu.CompilerParams(vmem_limit_bytes=40 * MIB),
        name="middle",
    )(got, keep, in_hbm(diag_values), in_hbm(column_values), in_hbm(row_values))
    reply = exchange(reply.reshape(devices, 8, 3 * width)).reshape(rows, 3 * width)

    return pl.pallas_call(
        functools.partial(tail_kernel, width),
        in_specs=[VM, HB, HB, HB, HB],
        out_specs=VM,
        out_shape=jax.ShapeDtypeStruct((row_count, width), BF),
        scratch_shapes=[
            pltpu.VMEM((row_count, 3 * rows), BF),
            pltpu.VMEM((row_count, hidden), F32),
            pltpu.VMEM((width, hidden), BF),
            pltpu.VMEM((hidden, width), BF),
            pltpu.VMEM((row_count, width), BF),
            pltpu.VMEM((row_count, width), F32),
            pltpu.SemaphoreType.DMA,
            pltpu.SemaphoreType.DMA((3, hidden // CHUNK)),
        ],
        compiler_params=pltpu.CompilerParams(vmem_limit_bytes=40 * MIB),
        name="tail",
    )(reply, in_hbm(gather), in_hbm(pre), in_hbm(up_weight), in_hbm(down_weight))


def solution(mesh):
    in_specs = (
        P(("arrow", "blk"), None),
        P(None, ("arrow", "blk")),
        P("arrow", "blk"),
        P("arrow", "blk"),
        P("arrow", "blk"),
        P(None, "arrow", "blk"),
        P(),
        P(),
    )
    out_specs = P(("arrow", "blk"), None)
    return jax.shard_map(body, mesh=mesh, in_specs=in_specs, out_specs=out_specs, check_vma=False)
```

```python
import functools

import jax
import jax.numpy as jnp
from jax import lax
from jax.experimental import pallas as pl
from jax.experimental.pallas import tpu as pltpu
from jax.sharding import PartitionSpec as P

BF = jnp.bfloat16
F32 = jnp.float32
VM = pl.BlockSpec(memory_space=pltpu.VMEM)
HB = pl.BlockSpec(memory_space=pltpu.HBM)
MIB = 1 << 20


def exchange(block):
    return lax.all_to_all(block, ("arrow", "blk"), split_axis=0, concat_axis=0, tiled=True)


def mm(a, b):
    return jnp.dot(a, b, preferred_element_type=F32)


def mm_nt(a, b):
    return lax.dot_general(a, b, (((1,), (1,)), ((), ())), preferred_element_type=F32)


def in_hbm(x):
    return pltpu.with_memory_space_constraint(x, pltpu.HBM)


def onehot(mask):
    return jnp.where(mask, 1.0, 0.0).astype(BF)


def pack_kernel(
    block_rows, width, feat_hbm, pos_hbm, out_hbm, feat_ref, pos_ref, out_ref, in_sem, out_sem
):
    nodes = feat_ref.shape[0]
    arrows = pos_ref.shape[0]
    rows = out_ref.shape[0] // arrows
    loads = (
        pltpu.make_async_copy(pos_hbm, pos_ref, in_sem.at[0]),
        pltpu.make_async_copy(feat_hbm, feat_ref, in_sem.at[1]),
    )
    for copy in loads:
        copy.start()
    n0 = lax.broadcasted_iota(jnp.int32, (nodes, nodes), 0)
    n1 = lax.broadcasted_iota(jnp.int32, (nodes, nodes), 1)
    before = onehot(n0 < n1)
    slot = lax.broadcasted_iota(jnp.int32, (rows, nodes), 0)
    r = slot % 8
    rf = r.astype(F32)
    shared = (r // 2 + 8).astype(F32)
    code_row = lax.broadcasted_iota(jnp.int32, (128, nodes), 0)
    for copy in loads:
        copy.wait()
    feats = feat_ref[...]

    def store(a):
        span = pl.ds(a * rows, rows)
        return pltpu.make_async_copy(out_ref.at[span, :], out_hbm.at[span, :], out_sem.at[a])

    for a in range(arrows):
        pos = pos_ref[a : a + 1, :]
        within = pos % block_rows
        member = pos // block_rows == slot // 8
        rank = jnp.where(member, mm(onehot(member), before), -1.0)
        head = jnp.broadcast_to(rank[0:1, :], rank.shape)
        picks = (
            onehot(rank == rf),
            onehot(jnp.where(r % 2 == 0, rank, head) == shared),
            onehot(head == rf),
        )
        high = (within // 32 + 1).astype(F32)
        low = (within % 32).astype(F32)
        span = pl.ds(a * rows, rows)
        codes = jnp.zeros((rows, 128), F32)
        for q in range(3):
            out_ref[span, q * width : (q + 1) * width] = mm(picks[q], feats).astype(BF)
            table = jnp.where(code_row == 2 * q, high, jnp.where(code_row == 2 * q + 1, low, 0.0))
            codes = codes + mm_nt(picks[q], table.astype(BF))
        out_ref[span, 3 * width :] = codes.astype(BF)
        store(a).start()
    for a in range(arrows):
        store(a).wait()


def prep_kernel(arrows, block_rows, width, pos_ref, feat_ref, w_ref, key_ref, pre_ref, up_ref):
    pre_ref[0] = mm(feat_ref[...], w_ref[:width, :]).astype(pre_ref.dtype)
    up_ref[0] = w_ref[width:, :]

    @pl.when(pl.program_id(0) == 0)
    def _():
        nodes = feat_ref.shape[0]
        n0 = lax.broadcasted_iota(jnp.int32, (nodes, nodes), 0)
        n1 = lax.broadcasted_iota(jnp.int32, (nodes, nodes), 1)
        before = onehot(n1 < n0)
        slot = lax.broadcasted_iota(jnp.int32, (nodes, 256), 1)
        lane = lax.broadcasted_iota(jnp.int32, (nodes, 128), 1)
        keys = jnp.zeros((nodes, 128), F32)
        for a in range(arrows):
            block = pos_ref[:, a : a + 1] // block_rows
            member = block == slot // 8
            rank = jnp.where(member & (slot % 8 == 0), mm(before, onehot(member)), 0.0)
            key = jnp.sum(rank, axis=1, keepdims=True) + (block * 16).astype(F32)
            keys = jnp.where(lane == a, key, keys)
        key_ref[...] = keys


def middle_kernel(
    width, got_ref, mask_ref, diag_hbm, col_hbm, row_hbm, out_hbm,
    w_ref, x_ref, x0_ref, y_ref, t_ref, p_ref, pt_ref, out_ref, s_ref, gm_ref, gh_ref, w_sem, out_sem,
):
    slots = got_ref.shape[0]
    size = x_ref.shape[0]
    half = slots // 2
    step = 256
    lanes = range(0, width, 128)
    loads = [
        pltpu.make_async_copy(src, w_ref.at[k], w_sem.at[k])
        for k, src in enumerate((diag_hbm, col_hbm, row_hbm))
    ]
    for copy in loads:
        copy.start()
    codes = got_ref[:, 3 * width :].astype(F32)
    place = (codes - 1.0) * 32.0 + pltpu.roll(codes, 127, 1)
    p_ref[0:slots, :] = place
    pt_ref[:, 0:slots] = place.T
    for j in lanes:
        s_ref[j // 128] = got_ref[:, width + j : width + j + 128].astype(F32)
    for k, ref in enumerate((gm_ref, gh_ref)):
        part = p_ref[pl.ds(k, half, stride=2), :]
        at = slots + k * half
        p_ref[at : at + half, :] = part
        pt_ref[:, at : at + half] = part.T
        for j in lanes:
            ref[:, j : j + 128] = s_ref[j // 128, pl.ds(k, half, stride=2), :].astype(BF)

    def unpack(c, carry):
        def put(row, start, count):
            ids = (lax.broadcasted_iota(jnp.int32, (step, count), 0) + c * step).astype(F32)
            return onehot(pt_ref[row : row + 1, start : start + count] == ids)

        span = pl.ds(pl.multiple_of(c * step, step), step)
        x_ref[span, :] = (
            mm(put(0, 0, slots), got_ref[:, 0:width]) + mm(put(2, slots, half), gm_ref[...])
        ).astype(BF)
        x0_ref[span, :] = (
            mm(put(4, 0, slots), got_ref[:, 2 * width : 3 * width])
            + mm(put(2, slots + half, half), gh_ref[...])
        ).astype(BF)
        return carry

    lax.fori_loop(0, size // step, unpack, 0)
    for copy in loads:
        copy.wait()
    tiles = mask_ref.shape[0] // 3
    edge = size // tiles
    for c in range(tiles):
        span = slice(c * edge, (c + 1) * edge)
        kept = []
        for k in range(3):
            keep = jnp.broadcast_to(mask_ref[k * tiles + c : k * tiles + c + 1, :], (edge, size))
            kept.append(w_ref[k, span, :] * keep.astype(BF))
        t_ref[span, :] = mm(kept[2], x_ref[...]).astype(BF)
        y_ref[span, :] = (mm(kept[0], x_ref[...]) + mm(kept[1], x0_ref[...])).astype(BF)

    def store(c):
        span = pl.ds(c * step, step)
        return pltpu.make_async_copy(out_ref.at[span, :], out_hbm.at[span, :], out_sem.at[c])

    for c in range(slots // step):
        span = slice(c * step, (c + 1) * step)

        def take(base, count, col):
            ids = lax.broadcasted_iota(jnp.int32, (count, size), 1).astype(F32)
            at = base + c * count
            return onehot(p_ref[at : at + count, col : col + 1] == ids)

        out_ref[span, 0:width] = mm(take(0, step, 0), y_ref[...]).astype(BF)
        even = mm(take(slots, step // 2, 2), y_ref[...])
        odd = mm(take(slots + half, step // 2, 2), t_ref[...])
        for j in lanes:
            s_ref[j // 128, pl.ds(0, step // 2, stride=2), :] = even[:, j : j + 128]
            s_ref[j // 128, pl.ds(1, step // 2, stride=2), :] = odd[:, j : j + 128]
            out_ref[span, width + j : width + j + 128] = s_ref[j // 128, 0:step, :].astype(BF)
        out_ref[span, 2 * width : 3 * width] = mm(take(0, step, 4), t_ref[...]).astype(BF)
        store(c).start()
    for c in range(slots // step):
        store(c).wait()


def tail_kernel(
    width, arrows, reply_ref, key_ref, pre_hbm, up_hbm, down_hbm, out_ref,
    pick_ref, pre_ref, up_ref, down_ref, agg_ref, acc_ref, sem,
):
    slots = reply_ref.shape[0]
    count, _, chunk = pre_ref.shape
    loads = []
    for c in range(count):
        span = pl.ds(c * chunk, chunk)
        loads.append(
            (
                pltpu.make_async_copy(up_hbm.at[c], up_ref.at[c], sem.at[0, c]),
                pltpu.make_async_copy(pre_hbm.at[c], pre_ref.at[c], sem.at[1, c]),
                pltpu.make_async_copy(down_hbm.at[span, :], down_ref.at[span, :], sem.at[2, c]),
            )
        )
        for copy in loads[c]:
            copy.start()
    rows = slots // arrows
    lane = lax.broadcasted_iota(jnp.int32, (1, rows), 1)
    block = lane // 8 * 16
    r = lane % 8
    goals = (block + r, jnp.where(r % 2 == 0, block, 0) + 8 + r // 2, r)
    total = jnp.zeros(agg_ref.shape, F32)
    for q in range(3):
        goal = goals[q].astype(F32)
        for a in range(arrows):
            pick_ref[:, a * rows : (a + 1) * rows] = onehot(key_ref[:, a : a + 1] == goal)
        total = total + mm(pick_ref[...], reply_ref[:, q * width : (q + 1) * width])
    agg_ref[...] = total.astype(BF)
    acc_ref[...] = jnp.zeros(acc_ref.shape, F32)
    for c in range(count):
        loads[c][0].wait()
        loads[c][1].wait()
        half = 0.5 * (pre_ref[c].astype(F32) + mm(agg_ref[...], up_ref[c]))
        hidden = (half * jnp.tanh(half) + half).astype(BF)
        loads[c][2].wait()
        acc_ref[...] += mm(hidden, down_ref[c * chunk : (c + 1) * chunk, :])
    out_ref[...] = acc_ref[...].astype(BF)


CHUNK = 1024
PRE = BF


def params(limit):
    return pltpu.CompilerParams(vmem_limit_bytes=limit * MIB)


def body(
    features, positions, diag_values, column_values, row_values, tile_masks, up_weight, down_weight
):
    row_count, width = features.shape
    arrows = positions.shape[0]
    devices = arrows * lax.axis_size("blk")
    size = diag_values.shape[0]
    hidden = down_weight.shape[0]
    tiles = tile_masks.shape[1]
    rows = devices * 8
    longest = 3 * width + 128
    count = hidden // CHUNK
    dma = pltpu.SemaphoreType.DMA

    message = pl.pallas_call(
        functools.partial(pack_kernel, size, width),
        in_specs=[HB, HB],
        out_specs=HB,
        out_shape=pltpu.HBM((rows, longest), BF),
        scratch_shapes=[
            pltpu.VMEM(features.shape, BF),
            pltpu.VMEM(positions.shape, jnp.int32),
            pltpu.VMEM((rows, longest), BF),
            dma((2,)),
            dma((arrows,)),
        ],
        compiler_params=params(24),
        name="pack",
    )(in_hbm(features), in_hbm(positions))
    got = exchange(message.reshape(devices, 8, longest)).reshape(rows, longest)

    key, pre, up = pl.pallas_call(
        functools.partial(prep_kernel, arrows, size, width),
        grid=(count,),
        in_specs=[
            pl.BlockSpec((row_count, arrows), lambda c: (0, 0)),
            pl.BlockSpec((row_count, width), lambda c: (0, 0)),
            pl.BlockSpec((2 * width, CHUNK), lambda c: (0, c)),
        ],
        out_specs=[
            pl.BlockSpec((row_count, 128), lambda c: (0, 0)),
            pl.BlockSpec((1, row_count, CHUNK), lambda c: (c, 0, 0)),
            pl.BlockSpec((1, width, CHUNK), lambda c: (c, 0, 0)),
        ],
        out_shape=[
            jax.ShapeDtypeStruct((row_count, 128), F32),
            pltpu.HBM((count, row_count, CHUNK), PRE),
            pltpu.HBM((count, width, CHUNK), BF),
        ],
        compiler_params=params(20),
        name="prep",
    )(positions.T, in_hbm(features), in_hbm(up_weight))
    keep = jnp.repeat(tile_masks.astype(F32), size // tiles, axis=2).reshape(3 * tiles, size)

    reply = pl.pallas_call(
        functools.partial(middle_kernel, width),
        in_specs=[VM, VM, HB, HB, HB],
        out_specs=HB,
        out_shape=pltpu.HBM((rows, 3 * width), BF),
        scratch_shapes=[pltpu.VMEM((3, size, size), BF)]
        + [pltpu.VMEM((size, width), BF)] * 4
        + [
            pltpu.VMEM((2 * rows, 128), F32),
            pltpu.VMEM((128, 2 * rows), F32),
            pltpu.VMEM((rows, 3 * width), BF),
            pltpu.VMEM((width // 128, rows, 128), F32),
            pltpu.VMEM((rows // 2, width), BF),
            pltpu.VMEM((rows // 2, width), BF),
            dma((3,)),
            dma((rows // 256,)),
        ],
        compiler_params=params(40),
        name="middle",
    )(got, keep, in_hbm(diag_values), in_hbm(column_values), in_hbm(row_values))
    reply = exchange(reply.reshape(devices, 8, 3 * width)).reshape(rows, 3 * width)

    return pl.pallas_call(
        functools.partial(tail_kernel, width, arrows),
        in_specs=[VM, VM, HB, HB, HB],
        out_specs=VM,
        out_shape=jax.ShapeDtypeStruct((row_count, width), BF),
        scratch_shapes=[
            pltpu.VMEM((row_count, rows), BF),
            pltpu.VMEM((count, row_count, CHUNK), PRE),
            pltpu.VMEM((count, width, CHUNK), BF),
            pltpu.VMEM((hidden, width), BF),
            pltpu.VMEM((row_count, width), BF),
            pltpu.VMEM((row_count, width), F32),
            dma((3, count)),
        ],
        compiler_params=params(40),
        name="tail",
    )(reply, key, in_hbm(pre), in_hbm(up), in_hbm(down_weight))


def solution(mesh):
    in_specs = (
        P(("arrow", "blk"), None),
        P(None, ("arrow", "blk")),
        P("arrow", "blk"),
        P("arrow", "blk"),
        P("arrow", "blk"),
        P(None, "arrow", "blk"),
        P(),
        P(),
    )
    out_specs = P(("arrow", "blk"), None)
    return jax.shard_map(body, mesh=mesh, in_specs=in_specs, out_specs=out_specs, check_vma=False)
```

```python
import functools

import jax
import jax.numpy as jnp
from jax import lax
from jax.experimental import pallas as pl
from jax.experimental.pallas import tpu as pltpu
from jax.sharding import PartitionSpec as P

BF = jnp.bfloat16
F32 = jnp.float32
VM = pl.BlockSpec(memory_space=pltpu.VMEM)
HB = pl.BlockSpec(memory_space=pltpu.HBM)
MIB = 1 << 20


def exchange(block):
    return lax.all_to_all(block, ("arrow", "blk"), split_axis=0, concat_axis=0, tiled=True)


def mm(a, b):
    return jnp.dot(a, b, preferred_element_type=F32)


def mm_nt(a, b):
    return lax.dot_general(a, b, (((1,), (1,)), ((), ())), preferred_element_type=F32)


def in_hbm(x):
    return pltpu.with_memory_space_constraint(x, pltpu.HBM)


def onehot(mask):
    return jnp.where(mask, 1.0, 0.0).astype(BF)


def pack_kernel(
    block_rows, width, feat_hbm, pos_hbm, out_hbm, feat_ref, pos_ref, out_ref, in_sem, out_sem
):
    nodes = feat_ref.shape[0]
    arrows = pos_ref.shape[0]
    rows = out_ref.shape[0] // arrows
    loads = (
        pltpu.make_async_copy(pos_hbm, pos_ref, in_sem.at[0]),
        pltpu.make_async_copy(feat_hbm, feat_ref, in_sem.at[1]),
    )
    for copy in loads:
        copy.start()
    n0 = lax.broadcasted_iota(jnp.int32, (nodes, nodes), 0)
    n1 = lax.broadcasted_iota(jnp.int32, (nodes, nodes), 1)
    before = onehot(n0 < n1)
    slot = lax.broadcasted_iota(jnp.int32, (rows, nodes), 0)
    r = slot % 8
    rf = r.astype(F32)
    shared = (r // 2 + 8).astype(F32)
    for copy in loads:
        copy.wait()
    feats = feat_ref[...]

    def store(a):
        span = pl.ds(a * rows, rows)
        return pltpu.make_async_copy(out_ref.at[span, :], out_hbm.at[span, :], out_sem.at[a])

    for a in range(arrows):
        member = pos_ref[a : a + 1, :] // block_rows == slot // 8
        rank = jnp.where(member, mm(onehot(member), before), -1.0)
        head = jnp.broadcast_to(rank[0:1, :], rank.shape)
        picks = (
            onehot(rank == rf),
            onehot(jnp.where(r % 2 == 0, rank, head) == shared),
            onehot(head == rf),
        )
        for q in range(3):
            out_ref[a * rows : (a + 1) * rows, q * width : (q + 1) * width] = mm(
                picks[q], feats
            ).astype(BF)
        store(a).start()
    for a in range(arrows):
        store(a).wait()


def places_kernel(blocks, block_rows, me_ref, table_ref, p_ref, pt_ref):
    sources, nodes = table_ref.shape
    slots = sources * 8
    half = slots // 2
    arrows = sources // blocks
    step = 256
    arrow = me_ref[0]
    block = me_ref[1]
    high = (table_ref[...] // 256).astype(F32).astype(BF)
    low = (table_ref[...] % 256).astype(F32).astype(BF)
    n0 = lax.broadcasted_iota(jnp.int32, (nodes, nodes), 0)
    n1 = lax.broadcasted_iota(jnp.int32, (nodes, nodes), 1)
    before = onehot(n0 < n1)

    def fill(c, carry):
        row = lax.broadcasted_iota(jnp.int32, (step, sources), 0) + c * step
        source = row // 8
        wanted = ((source % blocks) ^ block) * arrows + ((source // blocks) ^ arrow)
        spread = onehot(lax.broadcasted_iota(jnp.int32, (step, sources), 1) == wanted)
        pos = (mm(spread, high) * 256.0 + mm(spread, low)).astype(jnp.int32)
        r = lax.broadcasted_iota(jnp.int32, (step, nodes), 0) % 8
        rf = r.astype(F32)
        shared = (r // 2 + 8).astype(F32)
        within = (pos % block_rows + 1).astype(F32)
        member = pos // block_rows == block
        rank = jnp.where(member, mm(onehot(member), before), -1.0)
        member = pos // block_rows == 0
        head = jnp.where(member, mm(onehot(member), before), -1.0)
        lane = lax.broadcasted_iota(jnp.int32, (step, 128), 1)
        place = jnp.zeros((step, 128), F32)
        hits = (rank == rf, jnp.where(r % 2 == 0, rank, head) == shared, head == rf)
        for q in range(3):
            at = jnp.sum(jnp.where(hits[q], within, 0.0), axis=1, keepdims=True) - 1.0
            place = jnp.where(lane == 2 * q, at, place)
        p_ref[pl.ds(pl.multiple_of(c * step, step), step), :] = place
        return carry

    lax.fori_loop(0, slots // step, fill, 0)
    pt_ref[:, 0:slots] = p_ref[0:slots, :].T[0:8, :]
    for k in range(2):
        part = p_ref[pl.ds(k, half, stride=2), :]
        at = slots + k * half
        p_ref[at : at + half, :] = part
        pt_ref[:, at : at + half] = part.T[0:8, :]


def prep_kernel(arrows, block_rows, width, pos_ref, feat_ref, w_ref, key_ref, pre_ref, up_ref):
    pre_ref[0] = mm(feat_ref[...], w_ref[:width, :]).astype(pre_ref.dtype)
    up_ref[0] = w_ref[width:, :]

    @pl.when(pl.program_id(0) == 0)
    def _():
        nodes = feat_ref.shape[0]
        n0 = lax.broadcasted_iota(jnp.int32, (nodes, nodes), 0)
        n1 = lax.broadcasted_iota(jnp.int32, (nodes, nodes), 1)
        before = onehot(n1 < n0)
        slot = lax.broadcasted_iota(jnp.int32, (nodes, 256), 1)
        lane = lax.broadcasted_iota(jnp.int32, (nodes, 128), 1)
        keys = jnp.zeros((nodes, 128), F32)
        for a in range(arrows):
            block = pos_ref[:, a : a + 1] // block_rows
            member = block == slot // 8
            rank = jnp.where(member & (slot % 8 == 0), mm(before, onehot(member)), 0.0)
            key = jnp.sum(rank, axis=1, keepdims=True) + (block * 16).astype(F32)
            keys = jnp.where(lane == a, key, keys)
        key_ref[...] = keys


def middle_kernel(
    width, got_ref, pt_ref, mask_ref, p_hbm, diag_hbm, col_hbm, row_hbm, out_hbm,
    w_ref, x_ref, x0_ref, y_ref, t_ref, p_ref, out_ref, s_ref, gm_ref, gh_ref, w_sem, p_sem, out_sem,
):
    slots = got_ref.shape[0]
    size = x_ref.shape[0]
    half = slots // 2
    step = 256
    lanes = range(0, width, 128)
    loads = [
        pltpu.make_async_copy(src, w_ref.at[k], w_sem.at[k])
        for k, src in enumerate((diag_hbm, col_hbm, row_hbm))
    ]
    loads.append(pltpu.make_async_copy(p_hbm, p_ref, p_sem))
    for copy in loads:
        copy.start()
    for j in lanes:
        s_ref[j // 128] = got_ref[:, width + j : width + j + 128].astype(F32)
    for k, ref in enumerate((gm_ref, gh_ref)):
        for j in lanes:
            ref[:, j : j + 128] = s_ref[j // 128, pl.ds(k, half, stride=2), :].astype(BF)

    def unpack(c, carry):
        def put(row, start, count):
            ids = (lax.broadcasted_iota(jnp.int32, (step, count), 0) + c * step).astype(F32)
            return onehot(pt_ref[row : row + 1, start : start + count] == ids)

        span = pl.ds(pl.multiple_of(c * step, step), step)
        x_ref[span, :] = (
            mm(put(0, 0, slots), got_ref[:, 0:width]) + mm(put(2, slots, half), gm_ref[...])
        ).astype(BF)
        x0_ref[span, :] = (
            mm(put(4, 0, slots), got_ref[:, 2 * width : 3 * width])
            + mm(put(2, slots + half, half), gh_ref[...])
        ).astype(BF)
        return carry

    lax.fori_loop(0, size // step, unpack, 0)
    for copy in loads:
        copy.wait()
    tiles = mask_ref.shape[0] // 3
    edge = size // tiles
    for c in range(tiles):
        span = slice(c * edge, (c + 1) * edge)
        kept = []
        for k in range(3):
            keep = jnp.broadcast_to(mask_ref[k * tiles + c : k * tiles + c + 1, :], (edge, size))
            kept.append(w_ref[k, span, :] * keep.astype(BF))
        t_ref[span, :] = mm(kept[2], x_ref[...]).astype(BF)
        y_ref[span, :] = (mm(kept[0], x_ref[...]) + mm(kept[1], x0_ref[...])).astype(BF)

    def store(c):
        span = pl.ds(c * step, step)
        return pltpu.make_async_copy(out_ref.at[span, :], out_hbm.at[span, :], out_sem.at[c])

    for c in range(slots // step):
        span = slice(c * step, (c + 1) * step)

        def take(base, count, col):
            ids = lax.broadcasted_iota(jnp.int32, (count, size), 1).astype(F32)
            at = base + c * count
            return onehot(p_ref[at : at + count, col : col + 1] == ids)

        out_ref[span, 0:width] = mm(take(0, step, 0), y_ref[...]).astype(BF)
        even = mm(take(slots, step // 2, 2), y_ref[...])
        odd = mm(take(slots + half, step // 2, 2), t_ref[...])
        for j in lanes:
            s_ref[j // 128, pl.ds(0, step // 2, stride=2), :] = even[:, j : j + 128]
            s_ref[j // 128, pl.ds(1, step // 2, stride=2), :] = odd[:, j : j + 128]
            out_ref[span, width + j : width + j + 128] = s_ref[j // 128, 0:step, :].astype(BF)
        out_ref[span, 2 * width : 3 * width] = mm(take(0, step, 4), t_ref[...]).astype(BF)
        store(c).start()
    for c in range(slots // step):
        store(c).wait()


def tail_kernel(
    width, arrows, reply_ref, key_ref, pre_hbm, up_hbm, down_hbm, out_ref,
    pick_ref, pre_ref, up_ref, down_ref, agg_ref, acc_ref, sem,
):
    slots = reply_ref.shape[0]
    count, _, chunk = pre_ref.shape
    loads = []
    for c in range(count):
        span = pl.ds(c * chunk, chunk)
        loads.append(
            (
                pltpu.make_async_copy(up_hbm.at[c], up_ref.at[c], sem.at[0, c]),
                pltpu.make_async_copy(pre_hbm.at[c], pre_ref.at[c], sem.at[1, c]),
                pltpu.make_async_copy(down_hbm.at[span, :], down_ref.at[span, :], sem.at[2, c]),
            )
        )
        for copy in loads[c]:
            copy.start()
    rows = slots // arrows
    lane = lax.broadcasted_iota(jnp.int32, (1, rows), 1)
    block = lane // 8 * 16
    r = lane % 8
    goals = (block + r, jnp.where(r % 2 == 0, block, 0) + 8 + r // 2, r)
    total = jnp.zeros(agg_ref.shape, F32)
    for q in range(3):
        goal = goals[q].astype(F32)
        for a in range(arrows):
            pick_ref[:, a * rows : (a + 1) * rows] = onehot(key_ref[:, a : a + 1] == goal)
        total = total + mm(pick_ref[...], reply_ref[:, q * width : (q + 1) * width])
    agg_ref[...] = total.astype(BF)
    acc_ref[...] = jnp.zeros(acc_ref.shape, F32)
    for c in range(count):
        loads[c][0].wait()
        loads[c][1].wait()
        half = 0.5 * (pre_ref[c].astype(F32) + mm(agg_ref[...], up_ref[c]))
        hidden = (half * jnp.tanh(half) + half).astype(BF)
        loads[c][2].wait()
        acc_ref[...] += mm(hidden, down_ref[c * chunk : (c + 1) * chunk, :])
    out_ref[...] = acc_ref[...].astype(BF)


CHUNK = 1024
PRE = BF


def gather_positions(positions):
    arrows = positions.shape[0]
    blocks = lax.axis_size("blk")
    mine = lax.axis_index("arrow")

    def partner(x, axis, size, k):
        return lax.ppermute(x, axis, [(i, i ^ k) for i in range(size)])

    def pick(row):
        return lax.dynamic_slice_in_dim(positions, row, 1, 0)

    parts = [pick(mine)]
    for k in range(1, arrows):
        parts.append(partner(pick(mine ^ k), "arrow", arrows, k))
    table = jnp.concatenate(parts, axis=0)
    base = 1
    while base < blocks:
        fan = 2 if base == 1 else 4
        table = jnp.concatenate(
            [table] + [partner(table, "blk", blocks, base * k) for k in range(1, fan)], axis=0
        )
        base *= fan
    return table


def params(limit):
    return pltpu.CompilerParams(vmem_limit_bytes=limit * MIB)


def body(
    features, positions, diag_values, column_values, row_values, tile_masks, up_weight, down_weight
):
    row_count, width = features.shape
    arrows = positions.shape[0]
    devices = arrows * lax.axis_size("blk")
    size = diag_values.shape[0]
    hidden = down_weight.shape[0]
    tiles = tile_masks.shape[1]
    rows = devices * 8
    longest = 3 * width
    count = hidden // CHUNK
    dma = pltpu.SemaphoreType.DMA

    message = pl.pallas_call(
        functools.partial(pack_kernel, size, width),
        in_specs=[HB, HB],
        out_specs=HB,
        out_shape=pltpu.HBM((rows, longest), BF),
        scratch_shapes=[
            pltpu.VMEM(features.shape, BF),
            pltpu.VMEM(positions.shape, jnp.int32),
            pltpu.VMEM((rows, longest), BF),
            dma((2,)),
            dma((arrows,)),
        ],
        compiler_params=params(24),
        name="pack",
    )(in_hbm(features), in_hbm(positions))
    got = exchange(message.reshape(devices, 8, longest)).reshape(rows, longest)

    table = gather_positions(lax.optimization_barrier((positions, message))[0])
    me = jnp.stack([lax.axis_index("arrow"), lax.axis_index("blk")]).astype(jnp.int32)
    places, places_t = pl.pallas_call(
        functools.partial(places_kernel, devices // arrows, size),
        in_specs=[pl.BlockSpec(memory_space=pltpu.SMEM), VM],
        out_specs=[pl.BlockSpec((2 * rows, 128)), VM],
        out_shape=[pltpu.HBM((2 * rows, 128), F32), jax.ShapeDtypeStruct((8, 2 * rows), F32)],
        compiler_params=params(16),
        name="places",
    )(me, table)

    key, pre, up = pl.pallas_call(
        functools.partial(prep_kernel, arrows, size, width),
        grid=(count,),
        in_specs=[
            pl.BlockSpec((row_count, arrows), lambda c: (0, 0)),
            pl.BlockSpec((row_count, width), lambda c: (0, 0)),
            pl.BlockSpec((2 * width, CHUNK), lambda c: (0, c)),
        ],
        out_specs=[
            pl.BlockSpec((row_count, 128), lambda c: (0, 0)),
            pl.BlockSpec((1, row_count, CHUNK), lambda c: (c, 0, 0)),
            pl.BlockSpec((1, width, CHUNK), lambda c: (c, 0, 0)),
        ],
        out_shape=[
            jax.ShapeDtypeStruct((row_count, 128), F32),
            pltpu.HBM((count, row_count, CHUNK), PRE),
            pltpu.HBM((count, width, CHUNK), BF),
        ],
        compiler_params=params(20),
        name="prep",
    )(positions.T, in_hbm(features), in_hbm(up_weight))
    keep = jnp.repeat(tile_masks.astype(F32), size // tiles, axis=2).reshape(3 * tiles, size)

    reply = pl.pallas_call(
        functools.partial(middle_kernel, width),
        in_specs=[VM, VM, VM, HB, HB, HB, HB],
        out_specs=HB,
        out_shape=pltpu.HBM((rows, 3 * width), BF),
        scratch_shapes=[pltpu.VMEM((3, size, size), BF)]
        + [pltpu.VMEM((size, width), BF)] * 4
        + [
            pltpu.VMEM((2 * rows, 128), F32),
            pltpu.VMEM((rows, 3 * width), BF),
            pltpu.VMEM((width // 128, rows, 128), F32),
            pltpu.VMEM((rows // 2, width), BF),
            pltpu.VMEM((rows // 2, width), BF),
            dma((3,)),
            dma,
            dma((rows // 256,)),
        ],
        compiler_params=params(40),
        name="middle",
    )(got, places_t, keep, in_hbm(places), in_hbm(diag_values), in_hbm(column_values), in_hbm(row_values))
    reply = exchange(reply.reshape(devices, 8, 3 * width)).reshape(rows, 3 * width)

    return pl.pallas_call(
        functools.partial(tail_kernel, width, arrows),
        in_specs=[VM, VM, HB, HB, HB],
        out_specs=VM,
        out_shape=jax.ShapeDtypeStruct((row_count, width), BF),
        scratch_shapes=[
            pltpu.VMEM((row_count, rows), BF),
            pltpu.VMEM((count, row_count, CHUNK), PRE),
            pltpu.VMEM((count, width, CHUNK), BF),
            pltpu.VMEM((hidden, width), BF),
            pltpu.VMEM((row_count, width), BF),
            pltpu.VMEM((row_count, width), F32),
            dma((3, count)),
        ],
        compiler_params=params(40),
        name="tail",
    )(reply, key, in_hbm(pre), in_hbm(up), in_hbm(down_weight))


def solution(mesh):
    in_specs = (
        P(("arrow", "blk"), None),
        P(None, ("arrow", "blk")),
        P("arrow", "blk"),
        P("arrow", "blk"),
        P("arrow", "blk"),
        P(None, "arrow", "blk"),
        P(),
        P(),
    )
    out_specs = P(("arrow", "blk"), None)
    return jax.shard_map(body, mesh=mesh, in_specs=in_specs, out_specs=out_specs, check_vma=False)
```

```python
import functools

import jax
import jax.numpy as jnp
from jax import lax
from jax.experimental import pallas as pl
from jax.experimental.pallas import tpu as pltpu
from jax.sharding import PartitionSpec as P

BF = jnp.bfloat16
F32 = jnp.float32
VM = pl.BlockSpec(memory_space=pltpu.VMEM)
HB = pl.BlockSpec(memory_space=pltpu.HBM)
MIB = 1 << 20


def exchange(block):
    return lax.all_to_all(block, ("arrow", "blk"), split_axis=0, concat_axis=0, tiled=True)


def mm(a, b):
    return jnp.dot(a, b, preferred_element_type=F32)


def mm_nt(a, b):
    return lax.dot_general(a, b, (((1,), (1,)), ((), ())), preferred_element_type=F32)


def in_hbm(x):
    return pltpu.with_memory_space_constraint(x, pltpu.HBM)


def onehot(mask):
    return jnp.where(mask, 1.0, 0.0).astype(BF)


def pack_kernel(
    block_rows, width, feat_hbm, pos_hbm, out_hbm, feat_ref, pos_ref, out_ref, in_sem, out_sem
):
    nodes = feat_ref.shape[0]
    arrows = pos_ref.shape[0]
    rows = out_ref.shape[0] // arrows
    loads = (
        pltpu.make_async_copy(pos_hbm, pos_ref, in_sem.at[0]),
        pltpu.make_async_copy(feat_hbm, feat_ref, in_sem.at[1]),
    )
    for copy in loads:
        copy.start()
    n0 = lax.broadcasted_iota(jnp.int32, (nodes, nodes), 0)
    n1 = lax.broadcasted_iota(jnp.int32, (nodes, nodes), 1)
    before = onehot(n0 < n1)
    slot = lax.broadcasted_iota(jnp.int32, (rows, nodes), 0)
    r = slot % 8
    rf = r.astype(F32)
    shared = (r // 2 + 8).astype(F32)
    code_row = lax.broadcasted_iota(jnp.int32, (128, nodes), 0)
    for copy in loads:
        copy.wait()
    feats = feat_ref[...]

    def store(a):
        span = pl.ds(a * rows, rows)
        return pltpu.make_async_copy(out_ref.at[span, :], out_hbm.at[span, :], out_sem.at[a])

    for a in range(arrows):
        pos = pos_ref[a : a + 1, :]
        within = pos % block_rows
        member = pos // block_rows == slot // 8
        rank = jnp.where(member, mm(onehot(member), before), -1.0)
        head = jnp.broadcast_to(rank[0:1, :], rank.shape)
        picks = (
            onehot(rank == rf),
            onehot(jnp.where(r % 2 == 0, rank, head) == shared),
            onehot(head == rf),
        )
        high = (within // 32 + 1).astype(F32)
        low = (within % 32).astype(F32)
        span = pl.ds(a * rows, rows)
        codes = jnp.zeros((rows, 128), F32)
        for q in range(3):
            out_ref[span, q * width : (q + 1) * width] = mm(picks[q], feats).astype(BF)
            table = jnp.where(code_row == 2 * q, high, jnp.where(code_row == 2 * q + 1, low, 0.0))
            codes = codes + mm_nt(picks[q], table.astype(BF))
        out_ref[span, 3 * width :] = codes.astype(BF)
        store(a).start()
    for a in range(arrows):
        store(a).wait()


def prep_kernel(arrows, block_rows, width, pos_ref, feat_ref, w_ref, key_ref, pre_ref, up_ref):
    pre_ref[0] = mm(feat_ref[...], w_ref[:width, :]).astype(pre_ref.dtype)
    up_ref[0] = w_ref[width:, :]

    @pl.when(pl.program_id(0) == 0)
    def _():
        nodes = feat_ref.shape[0]
        n0 = lax.broadcasted_iota(jnp.int32, (nodes, nodes), 0)
        n1 = lax.broadcasted_iota(jnp.int32, (nodes, nodes), 1)
        before = onehot(n1 < n0)
        slot = lax.broadcasted_iota(jnp.int32, (nodes, 256), 1)
        lane = lax.broadcasted_iota(jnp.int32, (nodes, 128), 1)
        keys = jnp.zeros((nodes, 128), F32)
        for a in range(arrows):
            block = pos_ref[:, a : a + 1] // block_rows
            member = block == slot // 8
            rank = jnp.where(member & (slot % 8 == 0), mm(before, onehot(member)), 0.0)
            key = jnp.sum(rank, axis=1, keepdims=True) + (block * 16).astype(F32)
            keys = jnp.where(lane == a, key, keys)
        key_ref[...] = keys


STEP = 256


def keep_of(mask_ref, row, edge):
    return jnp.broadcast_to(mask_ref[row : row + 1, :], (edge, mask_ref.shape[1])).astype(BF)


def take(places):
    ids = lax.broadcasted_iota(jnp.int32, (places.shape[0], 1024), 1).astype(F32)
    return onehot(places == ids)


def arm_kernel(
    width, class_ref, got_ref, mask_ref, row_hbm,
    x_ref, t_ref, p_ref, pt_ref, gh_ref, own_ref, s0_ref, s1_ref, s2_ref, s3_ref,
    w_ref, s_ref, gm_ref, other_ref, w_sem,
):
    slots = got_ref.shape[0]
    size = x_ref.shape[0]
    half = slots // 2
    lanes = range(0, width, 128)
    load = pltpu.make_async_copy(row_hbm, w_ref, w_sem)
    load.start()
    codes = got_ref[:, 3 * width :].astype(F32)
    place = (codes - 1.0) * 32.0 + pltpu.roll(codes, 127, 1)
    p_ref[0:slots, :] = place
    pt_ref[:, 0:slots] = place.T[0:8, :]
    for j in lanes:
        s_ref[j // 128] = got_ref[:, width + j : width + j + 128].astype(F32)
    for k, ref in enumerate((gm_ref, gh_ref)):
        part = p_ref[pl.ds(k, half, stride=2), :]
        at = slots + k * half
        p_ref[at : at + half, :] = part
        pt_ref[:, at : at + half] = part.T[0:8, :]
        for j in lanes:
            ref[:, j : j + 128] = s_ref[j // 128, pl.ds(k, half, stride=2), :].astype(BF)
    first = class_ref[0] == 0
    for at, count, col, to in ((0, half, 4, 0), (slots + half, half // 2, 2, half)):
        even = p_ref[pl.ds(at, count, stride=2), :][:, col : col + 1]
        odd = p_ref[pl.ds(at + 1, count, stride=2), :][:, col : col + 1]
        own_ref[to : to + count, :] = jnp.broadcast_to(jnp.where(first, even, odd), (count, 128))
        other_ref[to : to + count, :] = jnp.broadcast_to(jnp.where(first, odd, even), (count, 128))

    def unpack(c, carry):
        def put(row, start, count):
            ids = (lax.broadcasted_iota(jnp.int32, (STEP, count), 0) + c * STEP).astype(F32)
            return onehot(pt_ref[row : row + 1, start : start + count] == ids)

        span = pl.ds(pl.multiple_of(c * STEP, STEP), STEP)
        x_ref[span, :] = (
            mm(put(0, 0, slots), got_ref[:, 0:width]) + mm(put(2, slots, half), gm_ref[...])
        ).astype(BF)
        return carry

    lax.fori_loop(0, size // STEP, unpack, 0)
    load.wait()
    tiles = mask_ref.shape[0] // 3
    edge = size // tiles
    for c in range(tiles):
        span = slice(c * edge, (c + 1) * edge)
        kept = w_ref[span, :] * keep_of(mask_ref, 2 * tiles + c, edge)
        t_ref[span, :] = mm(kept, x_ref[...]).astype(BF)
    n4 = half // 4
    n2 = half // 8
    for d, ref in enumerate((s0_ref, s1_ref, s2_ref, s3_ref)):
        ref[0:n4, :] = mm(take(other_ref[d * n4 : (d + 1) * n4, 0:1]), t_ref[...]).astype(BF)
        at = half + d * n2
        ref[n4:, :] = mm(take(other_ref[at : at + n2, 0:1]), t_ref[...]).astype(BF)


def block_kernel(
    width, got_ref, x_ref, t_ref, p_ref, pt_ref, gh_ref, own_ref, mask_ref, diag_hbm, col_hbm,
    out_hbm, extra_ref, arm_ref,
    w_ref, x0_ref, y_ref, out_ref, w_sem, out_sem,
):
    slots = got_ref.shape[0]
    size = x_ref.shape[0]
    half = slots // 2
    loads = [
        pltpu.make_async_copy(src, w_ref.at[k], w_sem.at[k])
        for k, src in enumerate((diag_hbm, col_hbm))
    ]
    for copy in loads:
        copy.start()

    def unpack(c, carry):
        def put(row, start, count):
            ids = (lax.broadcasted_iota(jnp.int32, (STEP, count), 0) + c * STEP).astype(F32)
            return onehot(pt_ref[row : row + 1, start : start + count] == ids)

        span = pl.ds(pl.multiple_of(c * STEP, STEP), STEP)
        x0_ref[span, :] = (
            mm(put(4, 0, slots), got_ref[:, 2 * width : 3 * width])
            + mm(put(2, slots + half, half), gh_ref[...])
        ).astype(BF)
        return carry

    lax.fori_loop(0, size // STEP, unpack, 0)
    for copy in loads:
        copy.wait()
    tiles = mask_ref.shape[0] // 3
    edge = size // tiles
    for c in range(tiles):
        span = slice(c * edge, (c + 1) * edge)
        diag = w_ref[0, span, :] * keep_of(mask_ref, c, edge)
        col = w_ref[1, span, :] * keep_of(mask_ref, tiles + c, edge)
        y_ref[span, :] = (mm(diag, x_ref[...]) + mm(col, x0_ref[...])).astype(BF)

    def store(c):
        span = pl.ds(c * STEP, STEP)
        return pltpu.make_async_copy(
            out_ref.at[span, :], out_hbm.at[span, pl.ds(0, width)], out_sem.at[c]
        )

    for c in range(slots // STEP):
        span = slice(c * STEP, (c + 1) * STEP)
        out_ref[span, :] = mm(take(p_ref[span, 0:1]), y_ref[...]).astype(BF)
        store(c).start()
    for c in range(half // STEP):
        span = slice(c * STEP, (c + 1) * STEP)
        extra_ref[span, :] = mm(
            take(p_ref[slots + c * STEP : slots + (c + 1) * STEP, 2:3]), y_ref[...]
        )
    for c in range(own_ref.shape[0] // STEP):
        span = slice(c * STEP, (c + 1) * STEP)
        arm_ref[span, :] = mm(take(own_ref[span, 0:1]), t_ref[...])
    for c in range(slots // STEP):
        store(c).wait()


def join_kernel(
    width, extra_ref, arm_ref, r0_ref, r1_ref, r2_ref, r3_ref, kept_hbm, out_hbm,
    out_ref, s_ref, e_ref, out_sem,
):
    slots = out_ref.shape[0]
    half = slots // 2
    n4 = half // 4
    n2 = half // 8

    def store(c):
        span = pl.ds(c * STEP, STEP)
        return pltpu.make_async_copy(
            out_ref.at[span, :], out_hbm.at[span, pl.ds(width, width + 128)], out_sem.at[c]
        )

    for d, ref in enumerate((r0_ref, r1_ref, r2_ref, r3_ref)):
        span = slice(d * STEP, (d + 1) * STEP)
        four = arm_ref[d * n4 : (d + 1) * n4, :] + ref[0:n4, :].astype(F32)
        at = half + d * n2
        two = arm_ref[at : at + n2, :] + ref[n4:, :].astype(F32)
        more = extra_ref[d * n4 : (d + 1) * n4, :]
        for j in range(0, width, 128):
            t = j // 128
            s_ref[d, t, pl.ds(0, n4, stride=2), :] = more[:, j : j + 128]
            s_ref[d, t, pl.ds(1, n4, stride=2), :] = four[:, j : j + 128]
            e_ref[d, pl.ds(t, n2, stride=4), :] = two[:, j : j + 128]
        for t in range(width // 128):
            out_ref[span, t * 128 : (t + 1) * 128] = s_ref[d, t].astype(BF)
        out_ref[span, width:] = e_ref[d].astype(BF)
        store(d).start()
    for d in range(4):
        store(d).wait()


def tail_kernel(
    width, arrows, reply_ref, key_ref, pre_hbm, up_hbm, down_hbm, out_ref,
    pick_ref, part_ref, pre_ref, up_ref, down_ref, agg_ref, acc_ref, sem,
):
    slots = reply_ref.shape[0]
    count, nodes, chunk = pre_ref.shape
    loads = []
    for c in range(count):
        span = pl.ds(c * chunk, chunk)
        loads.append(
            (
                pltpu.make_async_copy(up_hbm.at[c], up_ref.at[c], sem.at[0, c]),
                pltpu.make_async_copy(pre_hbm.at[c], pre_ref.at[c], sem.at[1, c]),
                pltpu.make_async_copy(down_hbm.at[span, :], down_ref.at[span, :], sem.at[2, c]),
            )
        )
        for copy in loads[c]:
            copy.start()
    rows = slots // arrows
    lane = lax.broadcasted_iota(jnp.int32, (1, rows), 1)
    blk = lane // 8
    block = blk * 16
    side = (blk // 8 + blk // 2) % 2
    r = lane % 8

    def hits(goal, a):
        return onehot(key_ref[:, a : a + 1] == goal.astype(F32))

    goals = (block + r, jnp.where(r % 2 == 0, block + 8 + r // 2, r - 1 + side))
    total = jnp.zeros(agg_ref.shape, F32)
    for q in range(2):
        for a in range(arrows):
            pick_ref[:, a * rows : (a + 1) * rows] = hits(goals[q], a)
        total = total + mm(pick_ref[...], reply_ref[:, q * width : (q + 1) * width])
    for t in range(width // 128):
        goal = jnp.where(r % 4 == t, 8 + r // 4 * 2 + side, -1)
        for a in range(arrows):
            part_ref[t * nodes : (t + 1) * nodes, a * rows : (a + 1) * rows] = hits(goal, a)
    rest = mm(part_ref[...], reply_ref[:, 2 * width :])
    for t in range(width // 128):
        span = slice(t * 128, (t + 1) * 128)
        agg_ref[:, span] = (total[:, span] + rest[t * nodes : (t + 1) * nodes, :]).astype(BF)
    acc_ref[...] = jnp.zeros(acc_ref.shape, F32)
    for c in range(count):
        loads[c][0].wait()
        loads[c][1].wait()
        half = 0.5 * (pre_ref[c].astype(F32) + mm(agg_ref[...], up_ref[c]))
        hidden = (half * jnp.tanh(half) + half).astype(BF)
        loads[c][2].wait()
        acc_ref[...] += mm(hidden, down_ref[c * chunk : (c + 1) * chunk, :])
    out_ref[...] = acc_ref[...].astype(BF)


CHUNK = 1024
PRE = BF


def neighbours(dx, dy):
    pairs = []
    for x in range(4):
        for y in range(4):
            for z in range(2):
                to = ((x + dx) % 4) * 8 + ((y + dy) % 4) * 2 + z
                pairs.append((x * 8 + y * 2 + z, to))
    return pairs


def params(limit):
    return pltpu.CompilerParams(vmem_limit_bytes=limit * MIB)


def body(
    features, positions, diag_values, column_values, row_values, tile_masks, up_weight, down_weight
):
    row_count, width = features.shape
    arrows = positions.shape[0]
    devices = arrows * lax.axis_size("blk")
    size = diag_values.shape[0]
    hidden = down_weight.shape[0]
    tiles = tile_masks.shape[1]
    rows = devices * 8
    longest = 3 * width + 128
    count = hidden // CHUNK
    dma = pltpu.SemaphoreType.DMA

    message = pl.pallas_call(
        functools.partial(pack_kernel, size, width),
        in_specs=[HB, HB],
        out_specs=HB,
        out_shape=pltpu.HBM((rows, longest), BF),
        scratch_shapes=[
            pltpu.VMEM(features.shape, BF),
            pltpu.VMEM(positions.shape, jnp.int32),
            pltpu.VMEM((rows, longest), BF),
            dma((2,)),
            dma((arrows,)),
        ],
        compiler_params=params(24),
        name="pack",
    )(in_hbm(features), in_hbm(positions))
    got = exchange(message.reshape(devices, 8, longest)).reshape(rows, longest)

    key, pre, up = pl.pallas_call(
        functools.partial(prep_kernel, arrows, size, width),
        grid=(count,),
        in_specs=[
            pl.BlockSpec((row_count, arrows), lambda c: (0, 0)),
            pl.BlockSpec((row_count, width), lambda c: (0, 0)),
            pl.BlockSpec((2 * width, CHUNK), lambda c: (0, c)),
        ],
        out_specs=[
            pl.BlockSpec((row_count, 128), lambda c: (0, 0)),
            pl.BlockSpec((1, row_count, CHUNK), lambda c: (c, 0, 0)),
            pl.BlockSpec((1, width, CHUNK), lambda c: (c, 0, 0)),
        ],
        out_shape=[
            jax.ShapeDtypeStruct((row_count, 128), F32),
            pltpu.HBM((count, row_count, CHUNK), PRE),
            pltpu.HBM((count, width, CHUNK), BF),
        ],
        compiler_params=params(20),
        name="prep",
    )(positions.T, in_hbm(features), in_hbm(up_weight))
    keep = jnp.repeat(tile_masks.astype(F32), size // tiles, axis=2).reshape(3 * tiles, size)

    blk = lax.axis_index("blk")
    side = ((blk // 8 + blk // 2) % 2).astype(jnp.int32).reshape(1)
    sm = pl.BlockSpec(memory_space=pltpu.SMEM)
    half = rows // 2
    part = jax.ShapeDtypeStruct((half // 4 + half // 8, width), BF)
    full = jax.ShapeDtypeStruct((size, width), BF)
    x, t, p, pt, gh, own, *given = pl.pallas_call(
        functools.partial(arm_kernel, width),
        in_specs=[sm, VM, VM, HB],
        out_specs=[VM] * 10,
        out_shape=[
            full,
            full,
            jax.ShapeDtypeStruct((2 * rows, 128), F32),
            jax.ShapeDtypeStruct((8, 2 * rows), F32),
            jax.ShapeDtypeStruct((half, width), BF),
            jax.ShapeDtypeStruct((half + half // 2, 128), F32),
            part,
            part,
            part,
            part,
        ],
        scratch_shapes=[
            pltpu.VMEM((size, size), BF),
            pltpu.VMEM((width // 128, rows, 128), F32),
            pltpu.VMEM((half, width), BF),
            pltpu.VMEM((half + half // 2, 128), F32),
            dma,
        ],
        compiler_params=params(16),
        name="arms",
    )(side, got, keep, in_hbm(row_values))
    taken = [
        lax.ppermute(g, "blk", neighbours(*move)) for g, move in zip(given, ((1, 0), (3, 0), (0, 1), (0, 3)))
    ]
    reply, extra, arm = pl.pallas_call(
        functools.partial(block_kernel, width),
        in_specs=[VM] * 8 + [HB, HB],
        out_specs=[HB, VM, VM],
        out_shape=[
            pltpu.HBM((rows, 2 * width + 128), BF),
            jax.ShapeDtypeStruct((half, width), F32),
            jax.ShapeDtypeStruct((half + half // 2, width), F32),
        ],
        scratch_shapes=[
            pltpu.VMEM((2, size, size), BF),
            pltpu.VMEM((size, width), BF),
            pltpu.VMEM((size, width), BF),
            pltpu.VMEM((rows, width), BF),
            dma((2,)),
            dma((rows // STEP,)),
        ],
        compiler_params=params(16),
        name="blocks",
    )(got, x, t, p, pt, gh, own, keep, in_hbm(diag_values), in_hbm(column_values))
    reply = pl.pallas_call(
        functools.partial(join_kernel, width),
        in_specs=[VM] * 6 + [HB],
        out_specs=HB,
        out_shape=pltpu.HBM((rows, 2 * width + 128), BF),
        input_output_aliases={6: 0},
        scratch_shapes=[
            pltpu.VMEM((rows, width + 128), BF),
            pltpu.VMEM((4, width // 128, STEP, 128), F32),
            pltpu.VMEM((4, STEP, 128), F32),
            dma((4,)),
        ],
        compiler_params=params(16),
        name="join",
    )(extra, arm, *taken, reply)
    reply = exchange(reply.reshape(devices, 8, 2 * width + 128)).reshape(rows, 2 * width + 128)

    return pl.pallas_call(
        functools.partial(tail_kernel, width, arrows),
        in_specs=[VM, VM, HB, HB, HB],
        out_specs=VM,
        out_shape=jax.ShapeDtypeStruct((row_count, width), BF),
        scratch_shapes=[
            pltpu.VMEM((row_count, rows), BF),
            pltpu.VMEM((row_count * (width // 128), rows), BF),
            pltpu.VMEM((count, row_count, CHUNK), PRE),
            pltpu.VMEM((count, width, CHUNK), BF),
            pltpu.VMEM((hidden, width), BF),
            pltpu.VMEM((row_count, width), BF),
            pltpu.VMEM((row_count, width), F32),
            dma((3, count)),
        ],
        compiler_params=params(40),
        name="tail",
    )(reply, key, in_hbm(pre), in_hbm(up), in_hbm(down_weight))


def solution(mesh):
    in_specs = (
        P(("arrow", "blk"), None),
        P(None, ("arrow", "blk")),
        P("arrow", "blk"),
        P("arrow", "blk"),
        P("arrow", "blk"),
        P(None, "arrow", "blk"),
        P(),
        P(),
    )
    out_specs = P(("arrow", "blk"), None)
    return jax.shard_map(body, mesh=mesh, in_specs=in_specs, out_specs=out_specs, check_vma=False)
```

```python
import functools

import jax
import jax.numpy as jnp
from jax import lax
from jax.experimental import pallas as pl
from jax.experimental.pallas import tpu as pltpu
from jax.sharding import PartitionSpec as P

BF = jnp.bfloat16
F32 = jnp.float32
VM = pl.BlockSpec(memory_space=pltpu.VMEM)
HB = pl.BlockSpec(memory_space=pltpu.HBM)
MIB = 1 << 20


def exchange(block):
    return lax.all_to_all(block, ("arrow", "blk"), split_axis=0, concat_axis=0, tiled=True)


def mm(a, b):
    return jnp.dot(a, b, preferred_element_type=F32)


def mm_nt(a, b):
    return lax.dot_general(a, b, (((1,), (1,)), ((), ())), preferred_element_type=F32)


def in_hbm(x):
    return pltpu.with_memory_space_constraint(x, pltpu.HBM)


def onehot(mask):
    return jnp.where(mask, 1.0, 0.0).astype(BF)


def pack_kernel(
    block_rows, width, feat_hbm, pos_hbm, out_hbm, feat_ref, pos_ref, out_ref, in_sem, out_sem
):
    nodes = feat_ref.shape[0]
    arrows = pos_ref.shape[0]
    rows = out_ref.shape[0] // arrows
    loads = (
        pltpu.make_async_copy(pos_hbm, pos_ref, in_sem.at[0]),
        pltpu.make_async_copy(feat_hbm, feat_ref, in_sem.at[1]),
    )
    for copy in loads:
        copy.start()
    n0 = lax.broadcasted_iota(jnp.int32, (nodes, nodes), 0)
    n1 = lax.broadcasted_iota(jnp.int32, (nodes, nodes), 1)
    before = onehot(n0 < n1)
    slot = lax.broadcasted_iota(jnp.int32, (rows, nodes), 0)
    r = slot % 8
    rf = r.astype(F32)
    shared = (r // 2 + 8).astype(F32)
    code_row = lax.broadcasted_iota(jnp.int32, (128, nodes), 0)
    for copy in loads:
        copy.wait()
    feats = feat_ref[...]

    def store(a):
        span = pl.ds(a * rows, rows)
        return pltpu.make_async_copy(out_ref.at[span, :], out_hbm.at[span, :], out_sem.at[a])

    for a in range(arrows):
        pos = pos_ref[a : a + 1, :]
        within = pos % block_rows
        member = pos // block_rows == slot // 8
        rank = jnp.where(member, mm(onehot(member), before), -1.0)
        head = jnp.broadcast_to(rank[0:1, :], rank.shape)
        picks = (
            onehot(rank == rf),
            onehot(jnp.where(r % 2 == 0, rank, head) == shared),
            onehot(head == rf),
        )
        high = (within // 32 + 1).astype(F32)
        low = (within % 32).astype(F32)
        span = pl.ds(a * rows, rows)
        codes = jnp.zeros((rows, 128), F32)
        for q in range(3):
            out_ref[span, q * width : (q + 1) * width] = mm(picks[q], feats).astype(BF)
            table = jnp.where(code_row == 2 * q, high, jnp.where(code_row == 2 * q + 1, low, 0.0))
            codes = codes + mm_nt(picks[q], table.astype(BF))
        out_ref[span, 3 * width :] = codes.astype(BF)
        store(a).start()
    for a in range(arrows):
        store(a).wait()


def prep_kernel(arrows, block_rows, width, pos_ref, feat_ref, w_ref, key_ref, pre_ref, up_ref):
    pre_ref[0] = mm(feat_ref[...], w_ref[:width, :]).astype(pre_ref.dtype)
    up_ref[0] = w_ref[width:, :]

    @pl.when(pl.program_id(0) == 0)
    def _():
        nodes = feat_ref.shape[0]
        n0 = lax.broadcasted_iota(jnp.int32, (nodes, nodes), 0)
        n1 = lax.broadcasted_iota(jnp.int32, (nodes, nodes), 1)
        before = onehot(n1 < n0)
        slot = lax.broadcasted_iota(jnp.int32, (nodes, 256), 1)
        lane = lax.broadcasted_iota(jnp.int32, (nodes, 128), 1)
        keys = jnp.zeros((nodes, 128), F32)
        for a in range(arrows):
            block = pos_ref[:, a : a + 1] // block_rows
            member = block == slot // 8
            rank = jnp.where(member & (slot % 8 == 0), mm(before, onehot(member)), 0.0)
            key = jnp.sum(rank, axis=1, keepdims=True) + (block * 16).astype(F32)
            keys = jnp.where(lane == a, key, keys)
        key_ref[...] = keys


STEP = 256


def keep_of(mask_ref, row, edge):
    return jnp.broadcast_to(mask_ref[row : row + 1, :], (edge, mask_ref.shape[1])).astype(BF)


def take(places):
    ids = lax.broadcasted_iota(jnp.int32, (places.shape[0], 1024), 1).astype(F32)
    return onehot(places == ids)


def arm_kernel(
    width, class_ref, got_ref, mask_ref, row_hbm,
    x_ref, t_ref, p_ref, pt_ref, gh_ref, own_ref, s0_ref, s1_ref,
    w_ref, s_ref, gm_ref, other_ref, w_sem,
):
    slots = got_ref.shape[0]
    size = x_ref.shape[0]
    half = slots // 2
    lanes = range(0, width, 128)
    load = pltpu.make_async_copy(row_hbm, w_ref, w_sem)
    load.start()
    codes = got_ref[:, 3 * width :].astype(F32)
    place = (codes - 1.0) * 32.0 + pltpu.roll(codes, 127, 1)
    p_ref[0:slots, :] = place
    pt_ref[:, 0:slots] = place.T[0:8, :]
    for j in lanes:
        s_ref[j // 128] = got_ref[:, width + j : width + j + 128].astype(F32)
    for k, ref in enumerate((gm_ref, gh_ref)):
        part = p_ref[pl.ds(k, half, stride=2), :]
        at = slots + k * half
        p_ref[at : at + half, :] = part
        pt_ref[:, at : at + half] = part.T[0:8, :]
        for j in lanes:
            ref[:, j : j + 128] = s_ref[j // 128, pl.ds(k, half, stride=2), :].astype(BF)
    first = class_ref[0] == 0
    for at, count, col, to in ((0, half, 4, 0), (slots + half, half // 2, 2, half)):
        even = p_ref[pl.ds(at, count, stride=2), :][:, col : col + 1]
        odd = p_ref[pl.ds(at + 1, count, stride=2), :][:, col : col + 1]
        own_ref[to : to + count, :] = jnp.broadcast_to(jnp.where(first, even, odd), (count, 128))
        other_ref[to : to + count, :] = jnp.broadcast_to(jnp.where(first, odd, even), (count, 128))

    def unpack(c, carry):
        def put(row, start, count):
            ids = (lax.broadcasted_iota(jnp.int32, (STEP, count), 0) + c * STEP).astype(F32)
            return onehot(pt_ref[row : row + 1, start : start + count] == ids)

        span = pl.ds(pl.multiple_of(c * STEP, STEP), STEP)
        x_ref[span, :] = (
            mm(put(0, 0, slots), got_ref[:, 0:width]) + mm(put(2, slots, half), gm_ref[...])
        ).astype(BF)
        return carry

    lax.fori_loop(0, size // STEP, unpack, 0)
    load.wait()
    tiles = mask_ref.shape[0] // 3
    edge = size // tiles
    for c in range(tiles):
        span = slice(c * edge, (c + 1) * edge)
        kept = w_ref[span, :] * keep_of(mask_ref, 2 * tiles + c, edge)
        t_ref[span, :] = mm(kept, x_ref[...]).astype(BF)
    n4 = half // 2
    n2 = half // 4
    for d, ref in enumerate((s0_ref, s1_ref)):
        ref[0:n4, :] = mm(take(other_ref[d * n4 : (d + 1) * n4, 0:1]), t_ref[...]).astype(BF)
        at = half + d * n2
        ref[n4:, :] = mm(take(other_ref[at : at + n2, 0:1]), t_ref[...]).astype(BF)


def block_kernel(
    width, got_ref, x_ref, t_ref, p_ref, pt_ref, gh_ref, own_ref, mask_ref, diag_hbm, col_hbm,
    out_hbm, extra_ref, arm_ref,
    w_ref, x0_ref, y_ref, out_ref, w_sem, out_sem,
):
    slots = got_ref.shape[0]
    size = x_ref.shape[0]
    half = slots // 2
    loads = [
        pltpu.make_async_copy(src, w_ref.at[k], w_sem.at[k])
        for k, src in enumerate((diag_hbm, col_hbm))
    ]
    for copy in loads:
        copy.start()

    def unpack(c, carry):
        def put(row, start, count):
            ids = (lax.broadcasted_iota(jnp.int32, (STEP, count), 0) + c * STEP).astype(F32)
            return onehot(pt_ref[row : row + 1, start : start + count] == ids)

        span = pl.ds(pl.multiple_of(c * STEP, STEP), STEP)
        x0_ref[span, :] = (
            mm(put(4, 0, slots), got_ref[:, 2 * width : 3 * width])
            + mm(put(2, slots + half, half), gh_ref[...])
        ).astype(BF)
        return carry

    lax.fori_loop(0, size // STEP, unpack, 0)
    for copy in loads:
        copy.wait()
    tiles = mask_ref.shape[0] // 3
    edge = size // tiles
    for c in range(tiles):
        span = slice(c * edge, (c + 1) * edge)
        diag = w_ref[0, span, :] * keep_of(mask_ref, c, edge)
        col = w_ref[1, span, :] * keep_of(mask_ref, tiles + c, edge)
        y_ref[span, :] = (mm(diag, x_ref[...]) + mm(col, x0_ref[...])).astype(BF)

    def store(c):
        span = pl.ds(c * STEP, STEP)
        return pltpu.make_async_copy(
            out_ref.at[span, :], out_hbm.at[span, pl.ds(0, width)], out_sem.at[c]
        )

    for c in range(slots // STEP):
        span = slice(c * STEP, (c + 1) * STEP)
        out_ref[span, :] = mm(take(p_ref[span, 0:1]), y_ref[...]).astype(BF)
        store(c).start()
    for c in range(half // STEP):
        span = slice(c * STEP, (c + 1) * STEP)
        extra_ref[span, :] = mm(
            take(p_ref[slots + c * STEP : slots + (c + 1) * STEP, 2:3]), y_ref[...]
        )
    for c in range(own_ref.shape[0] // STEP):
        span = slice(c * STEP, (c + 1) * STEP)
        arm_ref[span, :] = mm(take(own_ref[span, 0:1]), t_ref[...])
    for c in range(slots // STEP):
        store(c).wait()


def join_kernel(
    width, extra_ref, arm_ref, r0_ref, r1_ref, kept_hbm, out_hbm,
    out_ref, s_ref, e_ref, out_sem,
):
    slots = out_ref.shape[0]
    half = slots // 2
    n4 = half // 4
    n2 = half // 8

    def store(c):
        span = pl.ds(c * STEP, STEP)
        return pltpu.make_async_copy(
            out_ref.at[span, :], out_hbm.at[span, pl.ds(width, width + 128)], out_sem.at[c]
        )

    for d in range(4):
        ref = (r0_ref, r1_ref)[d // 2]
        span = slice(d * STEP, (d + 1) * STEP)
        at = d % 2 * n4
        four = arm_ref[d * n4 : (d + 1) * n4, :] + ref[at : at + n4, :].astype(F32)
        at = half + d * n2
        to = 2 * n4 + d % 2 * n2
        two = arm_ref[at : at + n2, :] + ref[to : to + n2, :].astype(F32)
        more = extra_ref[d * n4 : (d + 1) * n4, :]
        for j in range(0, width, 128):
            t = j // 128
            s_ref[d, t, pl.ds(0, n4, stride=2), :] = more[:, j : j + 128]
            s_ref[d, t, pl.ds(1, n4, stride=2), :] = four[:, j : j + 128]
            e_ref[d, pl.ds(t, n2, stride=4), :] = two[:, j : j + 128]
        for t in range(width // 128):
            out_ref[span, t * 128 : (t + 1) * 128] = s_ref[d, t].astype(BF)
        out_ref[span, width:] = e_ref[d].astype(BF)
        store(d).start()
    for d in range(4):
        store(d).wait()


def tail_kernel(
    width, arrows, reply_ref, key_ref, pre_hbm, up_hbm, down_hbm, out_ref,
    pick_ref, fold_ref, flat_ref, pre_ref, up_ref, down_ref, agg_ref, acc_ref, sem,
):
    slots = reply_ref.shape[0]
    count, nodes, chunk = pre_ref.shape
    loads = []
    for c in range(count):
        span = pl.ds(c * chunk, chunk)
        loads.append(
            (
                pltpu.make_async_copy(up_hbm.at[c], up_ref.at[c], sem.at[0, c]),
                pltpu.make_async_copy(pre_hbm.at[c], pre_ref.at[c], sem.at[1, c]),
                pltpu.make_async_copy(down_hbm.at[span, :], down_ref.at[span, :], sem.at[2, c]),
            )
        )
        for copy in loads[c]:
            copy.start()
    rows = slots // arrows
    lane = lax.broadcasted_iota(jnp.int32, (1, rows), 1)
    blk = lane // 8
    block = blk * 16
    side = (blk // 8 + blk // 2) % 2
    r = lane % 8

    def hits(goal, a):
        return onehot(key_ref[:, a : a + 1] == goal.astype(F32))

    goals = (block + r, jnp.where(r % 2 == 0, block + 8 + r // 2, r - 1 + side))
    total = jnp.zeros(agg_ref.shape, F32)
    for q in range(2):
        for a in range(arrows):
            pick_ref[:, a * rows : (a + 1) * rows] = hits(goals[q], a)
        total = total + mm(pick_ref[...], reply_ref[:, q * width : (q + 1) * width])
    folded = slots // 4
    fold_ref[...] = reply_ref[:, 2 * width :].astype(F32)
    for t in range(width // 128):
        flat_ref[:, t * 128 : (t + 1) * 128] = fold_ref[pl.ds(t, folded, stride=4), :].astype(BF)
    lane = lax.broadcasted_iota(jnp.int32, (1, folded), 1)
    per = folded // arrows
    blk = lane % per // 2
    goal = 8 + lane % 2 * 2 + (blk // 8 + blk // 2) % 2
    key = key_ref[:, 0:1]
    for a in range(1, arrows):
        key = jnp.where(lane >= a * per, key_ref[:, a : a + 1], key)
    total = total + mm(onehot(key == goal.astype(F32)), flat_ref[...])
    agg_ref[...] = total.astype(BF)
    acc_ref[...] = jnp.zeros(acc_ref.shape, F32)
    for c in range(count):
        loads[c][0].wait()
        loads[c][1].wait()
        half = 0.5 * (pre_ref[c].astype(F32) + mm(agg_ref[...], up_ref[c]))
        hidden = (half * jnp.tanh(half) + half).astype(BF)
        loads[c][2].wait()
        acc_ref[...] += mm(hidden, down_ref[c * chunk : (c + 1) * chunk, :])
    out_ref[...] = acc_ref[...].astype(BF)


CHUNK = 1024
PRE = BF


def neighbours(arrows, move):
    pairs = []
    for a in range(arrows):
        for x in range(4):
            for y in range(4):
                for z in range(2):
                    to_x = (x + move * (1 - a % 2)) % 4
                    to_y = (y + move * (a % 2)) % 4
                    pairs.append((a * 32 + x * 8 + y * 2 + z, a * 32 + to_x * 8 + to_y * 2 + z))
    return pairs


def params(limit):
    return pltpu.CompilerParams(vmem_limit_bytes=limit * MIB)


def body(
    features, positions, diag_values, column_values, row_values, tile_masks, up_weight, down_weight
):
    row_count, width = features.shape
    arrows = positions.shape[0]
    devices = arrows * lax.axis_size("blk")
    size = diag_values.shape[0]
    hidden = down_weight.shape[0]
    tiles = tile_masks.shape[1]
    rows = devices * 8
    longest = 3 * width + 128
    count = hidden // CHUNK
    dma = pltpu.SemaphoreType.DMA

    message = pl.pallas_call(
        functools.partial(pack_kernel, size, width),
        in_specs=[HB, HB],
        out_specs=HB,
        out_shape=pltpu.HBM((rows, longest), BF),
        scratch_shapes=[
            pltpu.VMEM(features.shape, BF),
            pltpu.VMEM(positions.shape, jnp.int32),
            pltpu.VMEM((rows, longest), BF),
            dma((2,)),
            dma((arrows,)),
        ],
        compiler_params=params(24),
        name="pack",
    )(in_hbm(features), in_hbm(positions))
    got = exchange(message.reshape(devices, 8, longest)).reshape(rows, longest)

    key, pre, up = pl.pallas_call(
        functools.partial(prep_kernel, arrows, size, width),
        grid=(count,),
        in_specs=[
            pl.BlockSpec((row_count, arrows), lambda c: (0, 0)),
            pl.BlockSpec((row_count, width), lambda c: (0, 0)),
            pl.BlockSpec((2 * width, CHUNK), lambda c: (0, c)),
        ],
        out_specs=[
            pl.BlockSpec((row_count, 128), lambda c: (0, 0)),
            pl.BlockSpec((1, row_count, CHUNK), lambda c: (c, 0, 0)),
            pl.BlockSpec((1, width, CHUNK), lambda c: (c, 0, 0)),
        ],
        out_shape=[
            jax.ShapeDtypeStruct((row_count, 128), F32),
            pltpu.HBM((count, row_count, CHUNK), PRE),
            pltpu.HBM((count, width, CHUNK), BF),
        ],
        compiler_params=params(20),
        name="prep",
    )(positions.T, in_hbm(features), in_hbm(up_weight))
    keep = jnp.repeat(tile_masks.astype(F32), size // tiles, axis=2).reshape(3 * tiles, size)

    blk = lax.axis_index("blk")
    side = ((blk // 8 + blk // 2) % 2).astype(jnp.int32).reshape(1)
    sm = pl.BlockSpec(memory_space=pltpu.SMEM)
    half = rows // 2
    part = jax.ShapeDtypeStruct((half // 2 + half // 4, width), BF)
    full = jax.ShapeDtypeStruct((size, width), BF)
    x, t, p, pt, gh, own, *given = pl.pallas_call(
        functools.partial(arm_kernel, width),
        in_specs=[sm, VM, VM, HB],
        out_specs=[VM] * 8,
        out_shape=[
            full,
            full,
            jax.ShapeDtypeStruct((2 * rows, 128), F32),
            jax.ShapeDtypeStruct((8, 2 * rows), F32),
            jax.ShapeDtypeStruct((half, width), BF),
            jax.ShapeDtypeStruct((half + half // 2, 128), F32),
            part,
            part,
        ],
        scratch_shapes=[
            pltpu.VMEM((size, size), BF),
            pltpu.VMEM((width // 128, rows, 128), F32),
            pltpu.VMEM((half, width), BF),
            pltpu.VMEM((half + half // 2, 128), F32),
            dma,
        ],
        compiler_params=params(16),
        name="arms",
    )(side, got, keep, in_hbm(row_values))
    taken = [
        lax.ppermute(g, ("arrow", "blk"), neighbours(arrows, move)) for g, move in zip(given, (1, 3))
    ]
    reply, extra, arm = pl.pallas_call(
        functools.partial(block_kernel, width),
        in_specs=[VM] * 8 + [HB, HB],
        out_specs=[HB, VM, VM],
        out_shape=[
            pltpu.HBM((rows, 2 * width + 128), BF),
            jax.ShapeDtypeStruct((half, width), F32),
            jax.ShapeDtypeStruct((half + half // 2, width), F32),
        ],
        scratch_shapes=[
            pltpu.VMEM((2, size, size), BF),
            pltpu.VMEM((size, width), BF),
            pltpu.VMEM((size, width), BF),
            pltpu.VMEM((rows, width), BF),
            dma((2,)),
            dma((rows // STEP,)),
        ],
        compiler_params=params(16),
        name="blocks",
    )(got, x, t, p, pt, gh, own, keep, in_hbm(diag_values), in_hbm(column_values))
    reply = pl.pallas_call(
        functools.partial(join_kernel, width),
        in_specs=[VM] * 4 + [HB],
        out_specs=HB,
        out_shape=pltpu.HBM((rows, 2 * width + 128), BF),
        input_output_aliases={4: 0},
        scratch_shapes=[
            pltpu.VMEM((rows, width + 128), BF),
            pltpu.VMEM((4, width // 128, STEP, 128), F32),
            pltpu.VMEM((4, STEP, 128), F32),
            dma((4,)),
        ],
        compiler_params=params(16),
        name="join",
    )(extra, arm, *taken, reply)
    reply = exchange(reply.reshape(devices, 8, 2 * width + 128)).reshape(rows, 2 * width + 128)

    return pl.pallas_call(
        functools.partial(tail_kernel, width, arrows),
        in_specs=[VM, VM, HB, HB, HB],
        out_specs=VM,
        out_shape=jax.ShapeDtypeStruct((row_count, width), BF),
        scratch_shapes=[
            pltpu.VMEM((row_count, rows), BF),
            pltpu.VMEM((rows, 128), F32),
            pltpu.VMEM((rows // 4, width), BF),
            pltpu.VMEM((count, row_count, CHUNK), PRE),
            pltpu.VMEM((count, width, CHUNK), BF),
            pltpu.VMEM((hidden, width), BF),
            pltpu.VMEM((row_count, width), BF),
            pltpu.VMEM((row_count, width), F32),
            dma((3, count)),
        ],
        compiler_params=params(40),
        name="tail",
    )(reply, key, in_hbm(pre), in_hbm(up), in_hbm(down_weight))


def solution(mesh):
    in_specs = (
        P(("arrow", "blk"), None),
        P(None, ("arrow", "blk")),
        P("arrow", "blk"),
        P("arrow", "blk"),
        P("arrow", "blk"),
        P(None, "arrow", "blk"),
        P(),
        P(),
    )
    out_specs = P(("arrow", "blk"), None)
    return jax.shard_map(body, mesh=mesh, in_specs=in_specs, out_specs=out_specs, check_vma=False)
```

```python
import functools

import jax
import jax.numpy as jnp
from jax import lax
from jax.experimental import pallas as pl
from jax.experimental.pallas import tpu as pltpu
from jax.sharding import PartitionSpec as P

BF = jnp.bfloat16
F32 = jnp.float32
VM = pl.BlockSpec(memory_space=pltpu.VMEM)
HB = pl.BlockSpec(memory_space=pltpu.HBM)
MIB = 1 << 20


def exchange(block):
    return lax.all_to_all(block, ("arrow", "blk"), split_axis=0, concat_axis=0, tiled=True)


def mm(a, b):
    return jnp.dot(a, b, preferred_element_type=F32)


def mm_nt(a, b):
    return lax.dot_general(a, b, (((1,), (1,)), ((), ())), preferred_element_type=F32)


def in_hbm(x):
    return pltpu.with_memory_space_constraint(x, pltpu.HBM)


def onehot(mask):
    return jnp.where(mask, 1.0, 0.0).astype(BF)


def side_of(blk):
    return (blk // 8 + blk // 2) % 2


def pack_kernel(
    block_rows, width, feat_hbm, pos_hbm, out_hbm,
    feat_ref, pos_ref, out_ref, fold_ref, in_sem, out_sem,
):
    nodes = feat_ref.shape[0]
    arrows = pos_ref.shape[0]
    rows = out_ref.shape[0] // arrows
    loads = (
        pltpu.make_async_copy(pos_hbm, pos_ref, in_sem.at[0]),
        pltpu.make_async_copy(feat_hbm, feat_ref, in_sem.at[1]),
    )
    for copy in loads:
        copy.start()
    n0 = lax.broadcasted_iota(jnp.int32, (nodes, nodes), 0)
    n1 = lax.broadcasted_iota(jnp.int32, (nodes, nodes), 1)
    before = onehot(n0 < n1)
    slot = lax.broadcasted_iota(jnp.int32, (rows, nodes), 0)
    r = slot % 8
    rf = r.astype(F32)
    side = side_of(slot // 8)
    shared = jnp.where(r % 2 == 0, r // 2 + 8, r - 1 + side).astype(F32)
    last = (8 + r // 4 * 2 + side).astype(F32)
    pair = lax.broadcasted_iota(jnp.int32, (rows // 4, nodes), 0)
    folded = (8 + pair % 2 * 2 + side_of(pair // 2)).astype(F32)
    code_row = lax.broadcasted_iota(jnp.int32, (128, nodes), 0)
    for copy in loads:
        copy.wait()
    feats = feat_ref[...]

    def store(a):
        span = pl.ds(a * rows, rows)
        return pltpu.make_async_copy(out_ref.at[span, :], out_hbm.at[span, :], out_sem.at[a])

    for a in range(arrows):
        pos = pos_ref[a : a + 1, :]
        within = pos % block_rows
        member = pos // block_rows == slot // 8
        rank = jnp.where(member, mm(onehot(member), before), -1.0)
        head = jnp.broadcast_to(rank[0:1, :], rank.shape)
        picks = (
            onehot(rank == rf),
            onehot(jnp.where(r % 2 == 0, rank, head) == shared),
            onehot(head == last),
        )
        high = (within // 32 + 1).astype(F32)
        low = (within % 32).astype(F32)
        span = pl.ds(a * rows, rows)
        codes = jnp.zeros((rows, 128), F32)
        rest = mm(onehot(head[0 : rows // 4, :] == folded), feats)
        for t in range(width // 128):
            fold_ref[a, pl.ds(t, rows // 4, stride=4), :] = rest[:, t * 128 : (t + 1) * 128]
        out_ref[span, 2 * width : 2 * width + 128] = fold_ref[a].astype(BF)
        for q in range(3):
            if q < 2:
                out_ref[span, q * width : (q + 1) * width] = mm(picks[q], feats).astype(BF)
            table = jnp.where(code_row == 2 * q, high, jnp.where(code_row == 2 * q + 1, low, 0.0))
            codes = codes + mm_nt(picks[q], table.astype(BF))
        out_ref[span, 2 * width + 128 :] = codes.astype(BF)
        store(a).start()
    for a in range(arrows):
        store(a).wait()


def prep_kernel(arrows, block_rows, width, pos_ref, feat_ref, w_ref, key_ref, pre_ref, up_ref):
    pre_ref[0] = mm(feat_ref[...], w_ref[:width, :]).astype(pre_ref.dtype)
    up_ref[0] = w_ref[width:, :]

    @pl.when(pl.program_id(0) == 0)
    def _():
        nodes = feat_ref.shape[0]
        n0 = lax.broadcasted_iota(jnp.int32, (nodes, nodes), 0)
        n1 = lax.broadcasted_iota(jnp.int32, (nodes, nodes), 1)
        before = onehot(n1 < n0)
        slot = lax.broadcasted_iota(jnp.int32, (nodes, 256), 1)
        lane = lax.broadcasted_iota(jnp.int32, (nodes, 128), 1)
        keys = jnp.zeros((nodes, 128), F32)
        for a in range(arrows):
            block = pos_ref[:, a : a + 1] // block_rows
            member = block == slot // 8
            rank = jnp.where(member & (slot % 8 == 0), mm(before, onehot(member)), 0.0)
            key = jnp.sum(rank, axis=1, keepdims=True) + (block * 16).astype(F32)
            keys = jnp.where(lane == a, key, keys)
        key_ref[...] = keys


STEP = 256


def keep_of(mask_ref, row, edge):
    return jnp.broadcast_to(mask_ref[row : row + 1, :], (edge, mask_ref.shape[1])).astype(BF)


def take(places):
    ids = lax.broadcasted_iota(jnp.int32, (places.shape[0], 1024), 1).astype(F32)
    return onehot(places == ids)


def head_kernel(width, got_ref, known_ref, e0_ref, e1_ref, p_ref, s_ref, f_ref):
    slots = got_ref.shape[0]
    four = slots // 4
    two = slots // 8
    group = four + two
    codes = got_ref[:, 2 * width + 128 :].astype(F32)
    p_ref[...] = (codes - 1.0) * 32.0 + pltpu.roll(codes, 127, 1)
    f_ref[...] = got_ref[:, 2 * width : 2 * width + 128].astype(F32)
    for t in range(width // 128):
        at = width + t * 128
        s_ref[t] = got_ref[:, at : at + 128].astype(F32)
    row = lax.broadcasted_iota(jnp.int32, (8, width), 0)
    for h, ref in enumerate((e0_ref, e1_ref)):
        base = h * (slots // 2)
        at = h * group
        some = p_ref[pl.ds(base + 1, four, stride=2), :][:, 2:3]
        known_ref[at : at + four, :] = jnp.broadcast_to(some, (four, 128))
        some = p_ref[pl.ds(base, two, stride=4), :][:, 4:5]
        known_ref[at + four : at + group, :] = jnp.broadcast_to(some, (two, 128))
        for t in range(width // 128):
            span = slice(t * 128, (t + 1) * 128)
            ref[0:four, span] = s_ref[t, pl.ds(base + 1, four, stride=2), :].astype(BF)
            ref[four:group, span] = f_ref[pl.ds(base + t, two, stride=4), :].astype(BF)
        place = known_ref[at : at + group, :].T[0:1, :]
        place = jnp.concatenate([place, jnp.zeros((1, width - group), F32)], axis=1)
        high = jnp.floor(place * (1.0 / 32.0)) + 1.0
        low = place - (high - 1.0) * 32.0
        ref[group:, :] = jnp.where(row == 0, high, jnp.where(row == 1, low, 0.0)).astype(BF)


def arm_kernel(
    width, got_ref, known_ref, mask_ref, row_hbm,
    x_ref, t_ref, p_ref, s0_ref, s1_ref,
    w_ref, pt_ref, s_ref, gm_ref, w_sem,
):
    slots = got_ref.shape[0]
    size = x_ref.shape[0]
    half = slots // 2
    lanes = range(0, width, 128)
    load = pltpu.make_async_copy(row_hbm, w_ref, w_sem)
    load.start()
    codes = got_ref[:, 2 * width + 128 :].astype(F32)
    place = (codes - 1.0) * 32.0 + pltpu.roll(codes, 127, 1)
    p_ref[0:slots, :] = place
    pt_ref[:, 0:slots] = place.T[0:8, :]
    part = p_ref[pl.ds(0, half, stride=2), :]
    p_ref[slots:, :] = part
    pt_ref[:, slots:] = part.T[0:8, :]
    for j in lanes:
        s_ref[j // 128] = got_ref[:, width + j : width + j + 128].astype(F32)
        gm_ref[:, j : j + 128] = s_ref[j // 128, pl.ds(0, half, stride=2), :].astype(BF)

    def unpack(c, carry):
        def put(row, start, count):
            ids = (lax.broadcasted_iota(jnp.int32, (STEP, count), 0) + c * STEP).astype(F32)
            return onehot(pt_ref[row : row + 1, start : start + count] == ids)

        span = pl.ds(pl.multiple_of(c * STEP, STEP), STEP)
        x_ref[span, :] = (
            mm(put(0, 0, slots), got_ref[:, 0:width]) + mm(put(2, slots, half), gm_ref[...])
        ).astype(BF)
        return carry

    lax.fori_loop(0, size // STEP, unpack, 0)
    load.wait()
    tiles = mask_ref.shape[0] // 3
    edge = size // tiles
    for c in range(tiles):
        span = slice(c * edge, (c + 1) * edge)
        kept = w_ref[span, :] * keep_of(mask_ref, 2 * tiles + c, edge)
        t_ref[span, :] = mm(kept, x_ref[...]).astype(BF)
    group = s0_ref.shape[0]
    for d, ref in enumerate((s0_ref, s1_ref)):
        ref[...] = mm(take(known_ref[d * group : (d + 1) * group, 0:1]), t_ref[...]).astype(BF)


def block_kernel(
    width, x_ref, t_ref, p_ref, e0_ref, e1_ref, f0_ref, f1_ref, mask_ref, diag_hbm, col_hbm,
    out_hbm, extra_ref, arm_ref,
    w_ref, x0_ref, y_ref, out_ref, g_ref, pt_ref, own_ref, w_sem, out_sem,
):
    slots = out_ref.shape[0]
    size = x_ref.shape[0]
    half = slots // 2
    loads = [
        pltpu.make_async_copy(src, w_ref.at[k], w_sem.at[k])
        for k, src in enumerate((diag_hbm, col_hbm))
    ]
    for copy in loads:
        copy.start()

    group = arm_ref.shape[0] // 2
    for i, ref in enumerate((e0_ref, e1_ref, f0_ref, f1_ref)):
        span = slice(i * group, (i + 1) * group)
        g_ref[span, :] = ref[0:group, :]
        codes = ref[group:, :].astype(F32)
        pt_ref[0:1, span] = ((codes[0:1, :] - 1.0) * 32.0 + codes[1:2, :])[:, 0:group]
    own_ref[...] = jnp.broadcast_to(pt_ref[0:1, 2 * group :], (128, 2 * group)).T

    def unpack(c, carry):
        ids = lax.broadcasted_iota(jnp.int32, (STEP, g_ref.shape[0]), 0) + c * STEP
        span = pl.ds(pl.multiple_of(c * STEP, STEP), STEP)
        x0_ref[span, :] = mm(onehot(pt_ref[0:1, :] == ids.astype(F32)), g_ref[...]).astype(BF)
        return carry

    lax.fori_loop(0, size // STEP, unpack, 0)
    for copy in loads:
        copy.wait()
    tiles = mask_ref.shape[0] // 3
    edge = size // tiles
    for c in range(tiles):
        span = slice(c * edge, (c + 1) * edge)
        diag = w_ref[0, span, :] * keep_of(mask_ref, c, edge)
        col = w_ref[1, span, :] * keep_of(mask_ref, tiles + c, edge)
        y_ref[span, :] = (mm(diag, x_ref[...]) + mm(col, x0_ref[...])).astype(BF)

    def store(c):
        span = pl.ds(c * STEP, STEP)
        return pltpu.make_async_copy(
            out_ref.at[span, :], out_hbm.at[span, pl.ds(0, width)], out_sem.at[c]
        )

    for c in range(slots // STEP):
        span = slice(c * STEP, (c + 1) * STEP)
        out_ref[span, :] = mm(take(p_ref[span, 0:1]), y_ref[...]).astype(BF)
        store(c).start()
    for c in range(half // STEP):
        span = slice(c * STEP, (c + 1) * STEP)
        extra_ref[span, :] = mm(
            take(p_ref[slots + c * STEP : slots + (c + 1) * STEP, 2:3]), y_ref[...]
        )
    for c in range(own_ref.shape[0] // STEP):
        span = slice(c * STEP, (c + 1) * STEP)
        arm_ref[span, :] = mm(take(own_ref[span, 0:1]), t_ref[...])
    for c in range(slots // STEP):
        store(c).wait()


def join_kernel(
    width, extra_ref, arm_ref, r0_ref, r1_ref, kept_hbm, out_hbm,
    out_ref, s_ref, e_ref, out_sem,
):
    slots = out_ref.shape[0]
    half = slots // 2
    n4 = half // 4
    n2 = half // 8

    def store(c):
        span = pl.ds(c * STEP, STEP)
        return pltpu.make_async_copy(
            out_ref.at[span, :], out_hbm.at[span, pl.ds(width, width + 128)], out_sem.at[c]
        )

    for d in range(4):
        ref = (r0_ref, r1_ref)[d // 2]
        span = slice(d * STEP, (d + 1) * STEP)
        base = d // 2 * ref.shape[0]
        at = d % 2 * n4
        four = arm_ref[base + at : base + at + n4, :] + ref[at : at + n4, :].astype(F32)
        at = 2 * n4 + d % 2 * n2
        two = arm_ref[base + at : base + at + n2, :] + ref[at : at + n2, :].astype(F32)
        more = extra_ref[d * n4 : (d + 1) * n4, :]
        for j in range(0, width, 128):
            t = j // 128
            s_ref[d, t, pl.ds(0, n4, stride=2), :] = more[:, j : j + 128]
            s_ref[d, t, pl.ds(1, n4, stride=2), :] = four[:, j : j + 128]
            e_ref[d, pl.ds(t, n2, stride=4), :] = two[:, j : j + 128]
        for t in range(width // 128):
            out_ref[span, t * 128 : (t + 1) * 128] = s_ref[d, t].astype(BF)
        out_ref[span, width:] = e_ref[d].astype(BF)
        store(d).start()
    for d in range(4):
        store(d).wait()


def tail_kernel(
    width, arrows, reply_ref, key_ref, pre_hbm, up_hbm, down_hbm, out_ref,
    pick_ref, fold_ref, flat_ref, pre_ref, up_ref, down_ref, agg_ref, acc_ref, sem,
):
    slots = reply_ref.shape[0]
    count, nodes, chunk = pre_ref.shape
    loads = []
    for c in range(count):
        span = pl.ds(c * chunk, chunk)
        loads.append(
            (
                pltpu.make_async_copy(up_hbm.at[c], up_ref.at[c], sem.at[0, c]),
                pltpu.make_async_copy(pre_hbm.at[c], pre_ref.at[c], sem.at[1, c]),
                pltpu.make_async_copy(down_hbm.at[span, :], down_ref.at[span, :], sem.at[2, c]),
            )
        )
        for copy in loads[c]:
            copy.start()
    rows = slots // arrows
    lane = lax.broadcasted_iota(jnp.int32, (1, rows), 1)
    blk = lane // 8
    block = blk * 16
    side = 1 - side_of(blk)
    r = lane % 8

    def hits(goal, a):
        return onehot(key_ref[:, a : a + 1] == goal.astype(F32))

    goals = (block + r, jnp.where(r % 2 == 0, block + 8 + r // 2, r - 1 + side))
    total = jnp.zeros(agg_ref.shape, F32)
    for q in range(2):
        for a in range(arrows):
            pick_ref[:, a * rows : (a + 1) * rows] = hits(goals[q], a)
        total = total + mm(pick_ref[...], reply_ref[:, q * width : (q + 1) * width])
    folded = slots // 4
    fold_ref[...] = reply_ref[:, 2 * width :].astype(F32)
    for t in range(width // 128):
        flat_ref[:, t * 128 : (t + 1) * 128] = fold_ref[pl.ds(t, folded, stride=4), :].astype(BF)
    lane = lax.broadcasted_iota(jnp.int32, (1, folded), 1)
    per = folded // arrows
    blk = lane % per // 2
    goal = 9 + lane % 2 * 2 - side_of(blk)
    key = key_ref[:, 0:1]
    for a in range(1, arrows):
        key = jnp.where(lane >= a * per, key_ref[:, a : a + 1], key)
    total = total + mm(onehot(key == goal.astype(F32)), flat_ref[...])
    agg_ref[...] = total.astype(BF)
    acc_ref[...] = jnp.zeros(acc_ref.shape, F32)
    for c in range(count):
        loads[c][0].wait()
        loads[c][1].wait()
        half = 0.5 * (pre_ref[c].astype(F32) + mm(agg_ref[...], up_ref[c]))
        hidden = (half * jnp.tanh(half) + half).astype(BF)
        loads[c][2].wait()
        acc_ref[...] += mm(hidden, down_ref[c * chunk : (c + 1) * chunk, :])
    out_ref[...] = acc_ref[...].astype(BF)


CHUNK = 1024
PRE = BF


def neighbours(arrows, move):
    pairs = []
    for a in range(arrows):
        for x in range(4):
            for y in range(4):
                for z in range(2):
                    to_x = (x + move * (1 - a % 2)) % 4
                    to_y = (y + move * (a % 2)) % 4
                    pairs.append((a * 32 + x * 8 + y * 2 + z, a * 32 + to_x * 8 + to_y * 2 + z))
    return pairs


def params(limit):
    return pltpu.CompilerParams(vmem_limit_bytes=limit * MIB)


def body(
    features, positions, diag_values, column_values, row_values, tile_masks, up_weight, down_weight
):
    row_count, width = features.shape
    arrows = positions.shape[0]
    devices = arrows * lax.axis_size("blk")
    size = diag_values.shape[0]
    hidden = down_weight.shape[0]
    tiles = tile_masks.shape[1]
    rows = devices * 8
    longest = 2 * width + 256
    count = hidden // CHUNK
    dma = pltpu.SemaphoreType.DMA

    message = pl.pallas_call(
        functools.partial(pack_kernel, size, width),
        in_specs=[HB, HB],
        out_specs=HB,
        out_shape=pltpu.HBM((rows, longest), BF),
        scratch_shapes=[
            pltpu.VMEM(features.shape, BF),
            pltpu.VMEM(positions.shape, jnp.int32),
            pltpu.VMEM((rows, longest), BF),
            pltpu.VMEM((arrows, rows // arrows, 128), F32),
            dma((2,)),
            dma((arrows,)),
        ],
        compiler_params=params(24),
        name="pack",
    )(in_hbm(features), in_hbm(positions))
    got = exchange(message.reshape(devices, 8, longest)).reshape(rows, longest)

    key, pre, up = pl.pallas_call(
        functools.partial(prep_kernel, arrows, size, width),
        grid=(count,),
        in_specs=[
            pl.BlockSpec((row_count, arrows), lambda c: (0, 0)),
            pl.BlockSpec((row_count, width), lambda c: (0, 0)),
            pl.BlockSpec((2 * width, CHUNK), lambda c: (0, c)),
        ],
        out_specs=[
            pl.BlockSpec((row_count, 128), lambda c: (0, 0)),
            pl.BlockSpec((1, row_count, CHUNK), lambda c: (c, 0, 0)),
            pl.BlockSpec((1, width, CHUNK), lambda c: (c, 0, 0)),
        ],
        out_shape=[
            jax.ShapeDtypeStruct((row_count, 128), F32),
            pltpu.HBM((count, row_count, CHUNK), PRE),
            pltpu.HBM((count, width, CHUNK), BF),
        ],
        compiler_params=params(20),
        name="prep",
    )(positions.T, in_hbm(features), in_hbm(up_weight))
    keep = jnp.repeat(tile_masks.astype(F32), size // tiles, axis=2).reshape(3 * tiles, size)

    half = rows // 2
    group = half // 2 + half // 4
    part = jax.ShapeDtypeStruct((group, width), BF)
    full = jax.ShapeDtypeStruct((size, width), BF)
    piece = jax.ShapeDtypeStruct((group + 8, width), BF)
    known, *heads = pl.pallas_call(
        functools.partial(head_kernel, width),
        in_specs=[VM],
        out_specs=[VM] * 3,
        out_shape=[jax.ShapeDtypeStruct((2 * group, 128), F32), piece, piece],
        scratch_shapes=[
            pltpu.VMEM((rows, 128), F32),
            pltpu.VMEM((width // 128, rows, 128), F32),
            pltpu.VMEM((rows, 128), F32),
        ],
        compiler_params=params(8),
        name="heads",
    )(got)
    moves = [neighbours(arrows, m) for m in (1, 3)]
    heads += [lax.ppermute(g, ("arrow", "blk"), m) for g, m in zip(heads, moves)]
    x, t, p, *given = pl.pallas_call(
        functools.partial(arm_kernel, width),
        in_specs=[VM, VM, VM, HB],
        out_specs=[VM] * 5,
        out_shape=[full, full, jax.ShapeDtypeStruct((rows + half, 128), F32), part, part],
        scratch_shapes=[
            pltpu.VMEM((size, size), BF),
            pltpu.VMEM((8, rows + half), F32),
            pltpu.VMEM((width // 128, rows, 128), F32),
            pltpu.VMEM((half, width), BF),
            dma,
        ],
        compiler_params=params(16),
        name="arms",
    )(got, known, keep, in_hbm(row_values))
    taken = [lax.ppermute(g, ("arrow", "blk"), m) for g, m in zip(given, moves)]
    reply, extra, arm = pl.pallas_call(
        functools.partial(block_kernel, width),
        in_specs=[VM] * 8 + [HB, HB],
        out_specs=[HB, VM, VM],
        out_shape=[
            pltpu.HBM((rows, 2 * width + 128), BF),
            jax.ShapeDtypeStruct((half, width), F32),
            jax.ShapeDtypeStruct((2 * group, width), F32),
        ],
        scratch_shapes=[
            pltpu.VMEM((2, size, size), BF),
            pltpu.VMEM((size, width), BF),
            pltpu.VMEM((size, width), BF),
            pltpu.VMEM((rows, width), BF),
            pltpu.VMEM((4 * group, width), BF),
            pltpu.VMEM((8, 4 * group), F32),
            pltpu.VMEM((2 * group, 128), F32),
            dma((2,)),
            dma((rows // STEP,)),
        ],
        compiler_params=params(16),
        name="blocks",
    )(x, t, p, *heads, keep, in_hbm(diag_values), in_hbm(column_values))
    reply = pl.pallas_call(
        functools.partial(join_kernel, width),
        in_specs=[VM] * 4 + [HB],
        out_specs=HB,
        out_shape=pltpu.HBM((rows, 2 * width + 128), BF),
        input_output_aliases={4: 0},
        scratch_shapes=[
            pltpu.VMEM((rows, width + 128), BF),
            pltpu.VMEM((4, width // 128, STEP, 128), F32),
            pltpu.VMEM((4, STEP, 128), F32),
            dma((4,)),
        ],
        compiler_params=params(16),
        name="join",
    )(extra, arm, *taken, reply)
    reply = exchange(reply.reshape(devices, 8, 2 * width + 128)).reshape(rows, 2 * width + 128)

    return pl.pallas_call(
        functools.partial(tail_kernel, width, arrows),
        in_specs=[VM, VM, HB, HB, HB],
        out_specs=VM,
        out_shape=jax.ShapeDtypeStruct((row_count, width), BF),
        scratch_shapes=[
            pltpu.VMEM((row_count, rows), BF),
            pltpu.VMEM((rows, 128), F32),
            pltpu.VMEM((rows // 4, width), BF),
            pltpu.VMEM((count, row_count, CHUNK), PRE),
            pltpu.VMEM((count, width, CHUNK), BF),
            pltpu.VMEM((hidden, width), BF),
            pltpu.VMEM((row_count, width), BF),
            pltpu.VMEM((row_count, width), F32),
            dma((3, count)),
        ],
        compiler_params=params(40),
        name="tail",
    )(reply, key, in_hbm(pre), in_hbm(up), in_hbm(down_weight))


def solution(mesh):
    in_specs = (
        P(("arrow", "blk"), None),
        P(None, ("arrow", "blk")),
        P("arrow", "blk"),
        P("arrow", "blk"),
        P("arrow", "blk"),
        P(None, "arrow", "blk"),
        P(),
        P(),
    )
    out_specs = P(("arrow", "blk"), None)
    return jax.shard_map(body, mesh=mesh, in_specs=in_specs, out_specs=out_specs, check_vma=False)
```

```python
import functools

import jax
import jax.numpy as jnp
from jax import lax
from jax.experimental import pallas as pl
from jax.experimental.pallas import tpu as pltpu
from jax.sharding import PartitionSpec as P

BF = jnp.bfloat16
F32 = jnp.float32
VM = pl.BlockSpec(memory_space=pltpu.VMEM)
HB = pl.BlockSpec(memory_space=pltpu.HBM)
MIB = 1 << 20


def exchange(block):
    return lax.all_to_all(block, ("arrow", "blk"), split_axis=0, concat_axis=0, tiled=True)


def mm(a, b):
    return jnp.dot(a, b, preferred_element_type=F32)


def mm_nt(a, b):
    return lax.dot_general(a, b, (((1,), (1,)), ((), ())), preferred_element_type=F32)


def in_hbm(x):
    return pltpu.with_memory_space_constraint(x, pltpu.HBM)


def onehot(mask):
    return jnp.where(mask, 1.0, 0.0).astype(BF)


def side_of(blk):
    return (blk // 8 + blk // 2) % 2


def pack_kernel(
    block_rows, width, feat_hbm, pos_hbm, out_hbm,
    feat_ref, pos_ref, out_ref, fold_ref, in_sem, out_sem,
):
    nodes = feat_ref.shape[0]
    arrows = pos_ref.shape[0]
    rows = out_ref.shape[0] // arrows
    loads = (
        pltpu.make_async_copy(pos_hbm, pos_ref, in_sem.at[0]),
        pltpu.make_async_copy(feat_hbm, feat_ref, in_sem.at[1]),
    )
    for copy in loads:
        copy.start()
    n0 = lax.broadcasted_iota(jnp.int32, (nodes, nodes), 0)
    n1 = lax.broadcasted_iota(jnp.int32, (nodes, nodes), 1)
    before = onehot(n0 < n1)
    slot = lax.broadcasted_iota(jnp.int32, (rows, nodes), 0)
    r = slot % 8
    rf = r.astype(F32)
    side = side_of(slot // 8)
    shared = jnp.where(r % 2 == 0, r // 2 + 8, r - 1 + side).astype(F32)
    last = (8 + r // 4 * 2 + side).astype(F32)
    pair = lax.broadcasted_iota(jnp.int32, (rows // 4, nodes), 0)
    folded = (8 + pair % 2 * 2 + side_of(pair // 2)).astype(F32)
    code_row = lax.broadcasted_iota(jnp.int32, (128, nodes), 0)
    for copy in loads:
        copy.wait()
    feats = feat_ref[...]

    def store(a):
        span = pl.ds(a * rows, rows)
        return pltpu.make_async_copy(out_ref.at[span, :], out_hbm.at[span, :], out_sem.at[a])

    for a in range(arrows):
        pos = pos_ref[a : a + 1, :]
        within = pos % block_rows
        member = pos // block_rows == slot // 8
        rank = jnp.where(member, mm(onehot(member), before), -1.0)
        head = jnp.broadcast_to(rank[0:1, :], rank.shape)
        picks = (
            onehot(rank == rf),
            onehot(jnp.where(r % 2 == 0, rank, head) == shared),
            onehot(head == last),
        )
        high = (within // 32 + 1).astype(F32)
        low = (within % 32).astype(F32)
        span = pl.ds(a * rows, rows)
        rest = mm(onehot(head[0 : rows // 4, :] == folded), feats)
        for t in range(width // 128):
            fold_ref[a, pl.ds(t, rows // 4, stride=4), :] = rest[:, t * 128 : (t + 1) * 128]
        out_ref[span, 2 * width : 2 * width + 128] = fold_ref[a].astype(BF)
        tables = []
        for q in range(3):
            if q < 2:
                out_ref[span, q * width : (q + 1) * width] = mm(picks[q], feats).astype(BF)
            table = jnp.where(code_row == 2 * q, high, jnp.where(code_row == 2 * q + 1, low, 0.0))
            tables.append(table.astype(BF))
        codes = mm_nt(jnp.concatenate(picks, axis=1), jnp.concatenate(tables, axis=1))
        out_ref[span, 2 * width + 128 :] = codes.astype(BF)
        store(a).start()
    for a in range(arrows):
        store(a).wait()


def prep_kernel(arrows, block_rows, width, pos_ref, feat_ref, w_ref, key_ref, pre_ref, up_ref):
    pre_ref[0] = mm(feat_ref[...], w_ref[:width, :]).astype(pre_ref.dtype)
    up_ref[0] = w_ref[width:, :]

    @pl.when(pl.program_id(0) == 0)
    def _():
        nodes = feat_ref.shape[0]
        n0 = lax.broadcasted_iota(jnp.int32, (nodes, nodes), 0)
        n1 = lax.broadcasted_iota(jnp.int32, (nodes, nodes), 1)
        before = onehot(n1 < n0)
        slot = lax.broadcasted_iota(jnp.int32, (nodes, 256), 1)
        lane = lax.broadcasted_iota(jnp.int32, (nodes, 128), 1)
        keys = jnp.zeros((nodes, 128), F32)
        for a in range(arrows):
            block = pos_ref[:, a : a + 1] // block_rows
            member = block == slot // 8
            rank = jnp.where(member & (slot % 8 == 0), mm(before, onehot(member)), 0.0)
            key = jnp.sum(rank, axis=1, keepdims=True) + (block * 16).astype(F32)
            keys = jnp.where(lane == a, key, keys)
        key_ref[...] = keys


STEP = 256
WIDE = 512


def keep_of(mask_ref, row, edge):
    return jnp.broadcast_to(mask_ref[row : row + 1, :], (edge, mask_ref.shape[1])).astype(BF)


def take(places):
    ids = lax.broadcasted_iota(jnp.int32, (places.shape[0], 1024), 1).astype(F32)
    return onehot(places == ids)


def head_kernel(width, got_ref, known_ref, e0_ref, e1_ref, p_ref, s_ref, f_ref):
    slots = got_ref.shape[0]
    four = slots // 4
    two = slots // 8
    group = four + two
    codes = got_ref[:, 2 * width + 128 :].astype(F32)
    p_ref[...] = (codes - 1.0) * 32.0 + pltpu.roll(codes, 127, 1)
    f_ref[...] = got_ref[:, 2 * width : 2 * width + 128].astype(F32)
    for t in range(width // 128):
        at = width + t * 128
        s_ref[t] = got_ref[:, at : at + 128].astype(F32)
    row = lax.broadcasted_iota(jnp.int32, (8, width), 0)
    for h, ref in enumerate((e0_ref, e1_ref)):
        base = h * (slots // 2)
        at = h * group
        some = p_ref[pl.ds(base + 1, four, stride=2), :][:, 2:3]
        known_ref[at : at + four, :] = jnp.broadcast_to(some, (four, 128))
        some = p_ref[pl.ds(base, two, stride=4), :][:, 4:5]
        known_ref[at + four : at + group, :] = jnp.broadcast_to(some, (two, 128))
        for t in range(width // 128):
            span = slice(t * 128, (t + 1) * 128)
            ref[0:four, span] = s_ref[t, pl.ds(base + 1, four, stride=2), :].astype(BF)
            ref[four:group, span] = f_ref[pl.ds(base + t, two, stride=4), :].astype(BF)
        place = known_ref[at : at + group, :].T[0:1, :]
        place = jnp.concatenate([place, jnp.zeros((1, width - group), F32)], axis=1)
        high = jnp.floor(place * (1.0 / 32.0)) + 1.0
        low = place - (high - 1.0) * 32.0
        ref[group:, :] = jnp.where(row == 0, high, jnp.where(row == 1, low, 0.0)).astype(BF)


def arm_kernel(
    width, got_ref, known_ref, mask_ref, row_hbm,
    x_ref, t_ref, p_ref, s0_ref, s1_ref,
    w_ref, pt_ref, s_ref, gm_ref, w_sem,
):
    slots = got_ref.shape[0]
    size = x_ref.shape[0]
    half = slots // 2
    lanes = range(0, width, 128)
    load = pltpu.make_async_copy(row_hbm, w_ref, w_sem)
    load.start()
    codes = got_ref[:, 2 * width + 128 :].astype(F32)
    place = (codes - 1.0) * 32.0 + pltpu.roll(codes, 127, 1)
    p_ref[0:slots, :] = place
    pt_ref[:, 0:slots] = place.T[0:8, :]
    part = p_ref[pl.ds(0, half, stride=2), :]
    p_ref[slots:, :] = part
    pt_ref[:, slots:] = part.T[0:8, :]
    for j in lanes:
        s_ref[j // 128] = got_ref[:, width + j : width + j + 128].astype(F32)
        gm_ref[:, j : j + 128] = s_ref[j // 128, pl.ds(0, half, stride=2), :].astype(BF)

    def unpack(c, carry):
        def put(row, start, count):
            ids = (lax.broadcasted_iota(jnp.int32, (WIDE, count), 0) + c * WIDE).astype(F32)
            return onehot(pt_ref[row : row + 1, start : start + count] == ids)

        span = pl.ds(pl.multiple_of(c * WIDE, WIDE), WIDE)
        x_ref[span, :] = (
            mm(put(0, 0, slots), got_ref[:, 0:width]) + mm(put(2, slots, half), gm_ref[...])
        ).astype(BF)
        return carry

    lax.fori_loop(0, size // WIDE, unpack, 0)
    load.wait()
    tiles = mask_ref.shape[0] // 3
    edge = size // tiles
    for c in range(0, tiles, 2):
        span = slice(c * edge, (c + 2) * edge)
        keep = [keep_of(mask_ref, 2 * tiles + c + i, edge) for i in range(2)]
        kept = w_ref[span, :] * jnp.concatenate(keep, axis=0)
        t_ref[span, :] = mm(kept, x_ref[...]).astype(BF)
    group = s0_ref.shape[0]
    for d, ref in enumerate((s0_ref, s1_ref)):
        ref[...] = mm(take(known_ref[d * group : (d + 1) * group, 0:1]), t_ref[...]).astype(BF)


def block_kernel(
    width, x_ref, t_ref, p_ref, e0_ref, e1_ref, f0_ref, f1_ref, mask_ref, diag_hbm, col_hbm,
    out_hbm, extra_ref, arm_ref,
    w_ref, x0_ref, y_ref, out_ref, g_ref, pt_ref, own_ref, w_sem, out_sem,
):
    slots = out_ref.shape[0]
    size = x_ref.shape[0]
    half = slots // 2
    loads = [
        pltpu.make_async_copy(src, w_ref.at[k], w_sem.at[k])
        for k, src in enumerate((diag_hbm, col_hbm))
    ]
    for copy in loads:
        copy.start()

    group = arm_ref.shape[0] // 2
    for i, ref in enumerate((e0_ref, e1_ref, f0_ref, f1_ref)):
        span = slice(i * group, (i + 1) * group)
        g_ref[span, :] = ref[0:group, :]
        codes = ref[group:, :].astype(F32)
        pt_ref[0:1, span] = ((codes[0:1, :] - 1.0) * 32.0 + codes[1:2, :])[:, 0:group]
    own_ref[...] = jnp.broadcast_to(pt_ref[0:1, 2 * group :], (128, 2 * group)).T

    def unpack(c, carry):
        ids = lax.broadcasted_iota(jnp.int32, (WIDE, g_ref.shape[0]), 0) + c * WIDE
        span = pl.ds(pl.multiple_of(c * WIDE, WIDE), WIDE)
        x0_ref[span, :] = mm(onehot(pt_ref[0:1, :] == ids.astype(F32)), g_ref[...]).astype(BF)
        return carry

    lax.fori_loop(0, size // WIDE, unpack, 0)
    for copy in loads:
        copy.wait()
    tiles = mask_ref.shape[0] // 3
    edge = size // tiles
    for c in range(tiles):
        span = slice(c * edge, (c + 1) * edge)
        diag = w_ref[0, span, :] * keep_of(mask_ref, c, edge)
        col = w_ref[1, span, :] * keep_of(mask_ref, tiles + c, edge)
        y_ref[span, :] = (mm(diag, x_ref[...]) + mm(col, x0_ref[...])).astype(BF)

    def store(c):
        span = pl.ds(c * STEP, STEP)
        return pltpu.make_async_copy(
            out_ref.at[span, :], out_hbm.at[span, pl.ds(0, width)], out_sem.at[c]
        )

    for c in range(slots // STEP):
        span = slice(c * STEP, (c + 1) * STEP)
        out_ref[span, :] = mm(take(p_ref[span, 0:1]), y_ref[...]).astype(BF)
        store(c).start()
    for c in range(half // STEP):
        span = slice(c * STEP, (c + 1) * STEP)
        extra_ref[span, :] = mm(
            take(p_ref[slots + c * STEP : slots + (c + 1) * STEP, 2:3]), y_ref[...]
        )
    for c in range(own_ref.shape[0] // STEP):
        span = slice(c * STEP, (c + 1) * STEP)
        arm_ref[span, :] = mm(take(own_ref[span, 0:1]), t_ref[...])
    for c in range(slots // STEP):
        store(c).wait()


def join_kernel(
    width, extra_ref, arm_ref, r0_ref, r1_ref, kept_hbm, out_hbm,
    out_ref, s_ref, e_ref, out_sem,
):
    slots = out_ref.shape[0]
    half = slots // 2
    n4 = half // 4
    n2 = half // 8

    def store(c):
        span = pl.ds(c * STEP, STEP)
        return pltpu.make_async_copy(
            out_ref.at[span, :], out_hbm.at[span, pl.ds(width, width + 128)], out_sem.at[c]
        )

    for d in range(4):
        ref = (r0_ref, r1_ref)[d // 2]
        span = slice(d * STEP, (d + 1) * STEP)
        base = d // 2 * ref.shape[0]
        at = d % 2 * n4
        four = arm_ref[base + at : base + at + n4, :] + ref[at : at + n4, :].astype(F32)
        at = 2 * n4 + d % 2 * n2
        two = arm_ref[base + at : base + at + n2, :] + ref[at : at + n2, :].astype(F32)
        more = extra_ref[d * n4 : (d + 1) * n4, :]
        for j in range(0, width, 128):
            t = j // 128
            s_ref[d, t, pl.ds(0, n4, stride=2), :] = more[:, j : j + 128]
            s_ref[d, t, pl.ds(1, n4, stride=2), :] = four[:, j : j + 128]
            e_ref[d, pl.ds(t, n2, stride=4), :] = two[:, j : j + 128]
        for t in range(width // 128):
            out_ref[span, t * 128 : (t + 1) * 128] = s_ref[d, t].astype(BF)
        out_ref[span, width:] = e_ref[d].astype(BF)
        store(d).start()
    for d in range(4):
        store(d).wait()


def tail_kernel(
    width, arrows, reply_ref, key_ref, pre_hbm, up_hbm, down_hbm, out_ref,
    pick_ref, fold_ref, flat_ref, pre_ref, up_ref, down_ref, agg_ref, acc_ref, sem,
):
    slots = reply_ref.shape[0]
    count, nodes, chunk = pre_ref.shape
    loads = []
    for c in range(count):
        span = pl.ds(c * chunk, chunk)
        loads.append(
            (
                pltpu.make_async_copy(up_hbm.at[c], up_ref.at[c], sem.at[0, c]),
                pltpu.make_async_copy(pre_hbm.at[c], pre_ref.at[c], sem.at[1, c]),
                pltpu.make_async_copy(down_hbm.at[span, :], down_ref.at[span, :], sem.at[2, c]),
            )
        )
        for copy in loads[c]:
            copy.start()
    rows = slots // arrows
    lane = lax.broadcasted_iota(jnp.int32, (1, rows), 1)
    blk = lane // 8
    block = blk * 16
    side = 1 - side_of(blk)
    r = lane % 8

    def hits(goal, a):
        return onehot(key_ref[:, a : a + 1] == goal.astype(F32))

    goals = (block + r, jnp.where(r % 2 == 0, block + 8 + r // 2, r - 1 + side))
    total = jnp.zeros(agg_ref.shape, F32)
    for q in range(2):
        for a in range(arrows):
            pick_ref[:, a * rows : (a + 1) * rows] = hits(goals[q], a)
        total = total + mm(pick_ref[...], reply_ref[:, q * width : (q + 1) * width])
    folded = slots // 4
    fold_ref[...] = reply_ref[:, 2 * width :].astype(F32)
    for t in range(width // 128):
        flat_ref[:, t * 128 : (t + 1) * 128] = fold_ref[pl.ds(t, folded, stride=4), :].astype(BF)
    lane = lax.broadcasted_iota(jnp.int32, (1, folded), 1)
    per = folded // arrows
    blk = lane % per // 2
    goal = 9 + lane % 2 * 2 - side_of(blk)
    key = key_ref[:, 0:1]
    for a in range(1, arrows):
        key = jnp.where(lane >= a * per, key_ref[:, a : a + 1], key)
    total = total + mm(onehot(key == goal.astype(F32)), flat_ref[...])
    agg_ref[...] = total.astype(BF)
    acc_ref[...] = jnp.zeros(acc_ref.shape, F32)
    for c in range(count):
        loads[c][0].wait()
        loads[c][1].wait()
        half = 0.5 * (pre_ref[c].astype(F32) + mm(agg_ref[...], up_ref[c]))
        hidden = (half * jnp.tanh(half) + half).astype(BF)
        loads[c][2].wait()
        acc_ref[...] += mm(hidden, down_ref[c * chunk : (c + 1) * chunk, :])
    out_ref[...] = acc_ref[...].astype(BF)


CHUNK = 1024
PRE = BF


def neighbours(arrows, move):
    pairs = []
    for a in range(arrows):
        for x in range(4):
            for y in range(4):
                for z in range(2):
                    to_x = (x + move * (1 - a % 2)) % 4
                    to_y = (y + move * (a % 2)) % 4
                    pairs.append((a * 32 + x * 8 + y * 2 + z, a * 32 + to_x * 8 + to_y * 2 + z))
    return pairs


def params(limit):
    return pltpu.CompilerParams(vmem_limit_bytes=limit * MIB)


def body(
    features, positions, diag_values, column_values, row_values, tile_masks, up_weight, down_weight
):
    row_count, width = features.shape
    arrows = positions.shape[0]
    devices = arrows * lax.axis_size("blk")
    size = diag_values.shape[0]
    hidden = down_weight.shape[0]
    tiles = tile_masks.shape[1]
    rows = devices * 8
    longest = 2 * width + 256
    count = hidden // CHUNK
    dma = pltpu.SemaphoreType.DMA

    message = pl.pallas_call(
        functools.partial(pack_kernel, size, width),
        in_specs=[HB, HB],
        out_specs=HB,
        out_shape=pltpu.HBM((rows, longest), BF),
        scratch_shapes=[
            pltpu.VMEM(features.shape, BF),
            pltpu.VMEM(positions.shape, jnp.int32),
            pltpu.VMEM((rows, longest), BF),
            pltpu.VMEM((arrows, rows // arrows, 128), F32),
            dma((2,)),
            dma((arrows,)),
        ],
        compiler_params=params(24),
        name="pack",
    )(in_hbm(features), in_hbm(positions))
    got = exchange(message.reshape(devices, 8, longest)).reshape(rows, longest)

    key, pre, up = pl.pallas_call(
        functools.partial(prep_kernel, arrows, size, width),
        grid=(count,),
        in_specs=[
            pl.BlockSpec((row_count, arrows), lambda c: (0, 0)),
            pl.BlockSpec((row_count, width), lambda c: (0, 0)),
            pl.BlockSpec((2 * width, CHUNK), lambda c: (0, c)),
        ],
        out_specs=[
            pl.BlockSpec((row_count, 128), lambda c: (0, 0)),
            pl.BlockSpec((1, row_count, CHUNK), lambda c: (c, 0, 0)),
            pl.BlockSpec((1, width, CHUNK), lambda c: (c, 0, 0)),
        ],
        out_shape=[
            jax.ShapeDtypeStruct((row_count, 128), F32),
            pltpu.HBM((count, row_count, CHUNK), PRE),
            pltpu.HBM((count, width, CHUNK), BF),
        ],
        compiler_params=params(20),
        name="prep",
    )(positions.T, in_hbm(features), in_hbm(up_weight))
    keep = jnp.repeat(tile_masks.astype(F32), size // tiles, axis=2).reshape(3 * tiles, size)

    half = rows // 2
    group = half // 2 + half // 4
    part = jax.ShapeDtypeStruct((group, width), BF)
    full = jax.ShapeDtypeStruct((size, width), BF)
    piece = jax.ShapeDtypeStruct((group + 8, width), BF)
    known, *heads = pl.pallas_call(
        functools.partial(head_kernel, width),
        in_specs=[VM],
        out_specs=[VM] * 3,
        out_shape=[jax.ShapeDtypeStruct((2 * group, 128), F32), piece, piece],
        scratch_shapes=[
            pltpu.VMEM((rows, 128), F32),
            pltpu.VMEM((width // 128, rows, 128), F32),
            pltpu.VMEM((rows, 128), F32),
        ],
        compiler_params=params(8),
        name="heads",
    )(got)
    moves = [neighbours(arrows, m) for m in (1, 3)]
    heads += [lax.ppermute(g, ("arrow", "blk"), m) for g, m in zip(heads, moves)]
    x, t, p, *given = pl.pallas_call(
        functools.partial(arm_kernel, width),
        in_specs=[VM, VM, VM, HB],
        out_specs=[VM] * 5,
        out_shape=[full, full, jax.ShapeDtypeStruct((rows + half, 128), F32), part, part],
        scratch_shapes=[
            pltpu.VMEM((size, size), BF),
            pltpu.VMEM((8, rows + half), F32),
            pltpu.VMEM((width // 128, rows, 128), F32),
            pltpu.VMEM((half, width), BF),
            dma,
        ],
        compiler_params=params(16),
        name="arms",
    )(got, known, keep, in_hbm(row_values))
    taken = [lax.ppermute(g, ("arrow", "blk"), m) for g, m in zip(given, moves)]
    reply, extra, arm = pl.pallas_call(
        functools.partial(block_kernel, width),
        in_specs=[VM] * 8 + [HB, HB],
        out_specs=[HB, VM, VM],
        out_shape=[
            pltpu.HBM((rows, 2 * width + 128), BF),
            jax.ShapeDtypeStruct((half, width), F32),
            jax.ShapeDtypeStruct((2 * group, width), F32),
        ],
        scratch_shapes=[
            pltpu.VMEM((2, size, size), BF),
            pltpu.VMEM((size, width), BF),
            pltpu.VMEM((size, width), BF),
            pltpu.VMEM((rows, width), BF),
            pltpu.VMEM((4 * group, width), BF),
            pltpu.VMEM((8, 4 * group), F32),
            pltpu.VMEM((2 * group, 128), F32),
            dma((2,)),
            dma((rows // STEP,)),
        ],
        compiler_params=params(16),
        name="blocks",
    )(x, t, p, *heads, keep, in_hbm(diag_values), in_hbm(column_values))
    reply = pl.pallas_call(
        functools.partial(join_kernel, width),
        in_specs=[VM] * 4 + [HB],
        out_specs=HB,
        out_shape=pltpu.HBM((rows, 2 * width + 128), BF),
        input_output_aliases={4: 0},
        scratch_shapes=[
            pltpu.VMEM((rows, width + 128), BF),
            pltpu.VMEM((4, width // 128, STEP, 128), F32),
            pltpu.VMEM((4, STEP, 128), F32),
            dma((4,)),
        ],
        compiler_params=params(16),
        name="join",
    )(extra, arm, *taken, reply)
    reply = exchange(reply.reshape(devices, 8, 2 * width + 128)).reshape(rows, 2 * width + 128)

    return pl.pallas_call(
        functools.partial(tail_kernel, width, arrows),
        in_specs=[VM, VM, HB, HB, HB],
        out_specs=VM,
        out_shape=jax.ShapeDtypeStruct((row_count, width), BF),
        scratch_shapes=[
            pltpu.VMEM((row_count, rows), BF),
            pltpu.VMEM((rows, 128), F32),
            pltpu.VMEM((rows // 4, width), BF),
            pltpu.VMEM((count, row_count, CHUNK), PRE),
            pltpu.VMEM((count, width, CHUNK), BF),
            pltpu.VMEM((hidden, width), BF),
            pltpu.VMEM((row_count, width), BF),
            pltpu.VMEM((row_count, width), F32),
            dma((3, count)),
        ],
        compiler_params=params(40),
        name="tail",
    )(reply, key, in_hbm(pre), in_hbm(up), in_hbm(down_weight))


def solution(mesh):
    in_specs = (
        P(("arrow", "blk"), None),
        P(None, ("arrow", "blk")),
        P("arrow", "blk"),
        P("arrow", "blk"),
        P("arrow", "blk"),
        P(None, "arrow", "blk"),
        P(),
        P(),
    )
    out_specs = P(("arrow", "blk"), None)
    return jax.shard_map(body, mesh=mesh, in_specs=in_specs, out_specs=out_specs, check_vma=False)
```

```python
import functools

import jax
import jax.numpy as jnp
from jax import lax
from jax.experimental import pallas as pl
from jax.experimental.pallas import tpu as pltpu
from jax.sharding import PartitionSpec as P

BF = jnp.bfloat16
F32 = jnp.float32
VM = pl.BlockSpec(memory_space=pltpu.VMEM)
HB = pl.BlockSpec(memory_space=pltpu.HBM)
MIB = 1 << 20


def exchange(block):
    return lax.all_to_all(block, ("arrow", "blk"), split_axis=0, concat_axis=0, tiled=True)


def mm(a, b):
    return jnp.dot(a, b, preferred_element_type=F32)


def mm_nt(a, b):
    return lax.dot_general(a, b, (((1,), (1,)), ((), ())), preferred_element_type=F32)


def in_hbm(x):
    return pltpu.with_memory_space_constraint(x, pltpu.HBM)


def onehot(mask):
    return jnp.where(mask, 1.0, 0.0).astype(BF)


def side_of(blk):
    return (blk // 8 + blk // 2) % 2


def pack_kernel(
    block_rows, width, feat_hbm, pos_hbm, out_hbm,
    feat_ref, pos_ref, out_ref, fold_ref, in_sem, out_sem,
):
    nodes = feat_ref.shape[0]
    arrows = pos_ref.shape[0]
    rows = out_ref.shape[0] // arrows
    loads = (
        pltpu.make_async_copy(pos_hbm, pos_ref, in_sem.at[0]),
        pltpu.make_async_copy(feat_hbm, feat_ref, in_sem.at[1]),
    )
    for copy in loads:
        copy.start()
    n0 = lax.broadcasted_iota(jnp.int32, (nodes, nodes), 0)
    n1 = lax.broadcasted_iota(jnp.int32, (nodes, nodes), 1)
    before = onehot(n0 < n1)
    slot = lax.broadcasted_iota(jnp.int32, (rows, nodes), 0)
    r = slot % 8
    rf = r.astype(F32)
    side = side_of(slot // 8)
    shared = jnp.where(r % 2 == 0, r // 2 + 8, r - 1 + side).astype(F32)
    last = (8 + r // 4 * 2 + side).astype(F32)
    pair = lax.broadcasted_iota(jnp.int32, (rows // 4, nodes), 0)
    folded = (8 + pair % 2 * 2 + side_of(pair // 2)).astype(F32)
    code_row = lax.broadcasted_iota(jnp.int32, (128, nodes), 0)
    for copy in loads:
        copy.wait()
    feats = feat_ref[...]

    def store(a):
        span = pl.ds(a * rows, rows)
        return pltpu.make_async_copy(out_ref.at[span, :], out_hbm.at[span, :], out_sem.at[a])

    for a in range(arrows):
        pos = pos_ref[a : a + 1, :]
        within = pos % block_rows
        member = pos // block_rows == slot // 8
        rank = jnp.where(member, mm(onehot(member), before), -1.0)
        head = jnp.broadcast_to(rank[0:1, :], rank.shape)
        picks = (
            onehot(rank == rf),
            onehot(jnp.where(r % 2 == 0, rank, head) == shared),
            onehot(head == last),
        )
        high = (within // 32 + 1).astype(F32)
        low = (within % 32).astype(F32)
        span = pl.ds(a * rows, rows)
        rest = mm(onehot(head[0 : rows // 4, :] == folded), feats)
        for t in range(width // 128):
            fold_ref[a, pl.ds(t, rows // 4, stride=4), :] = rest[:, t * 128 : (t + 1) * 128]
        out_ref[span, 2 * width : 2 * width + 128] = fold_ref[a].astype(BF)
        tables = []
        for q in range(3):
            if q < 2:
                out_ref[span, q * width : (q + 1) * width] = mm(picks[q], feats).astype(BF)
            table = jnp.where(code_row == 2 * q, high, jnp.where(code_row == 2 * q + 1, low, 0.0))
            tables.append(table.astype(BF))
        codes = mm_nt(jnp.concatenate(picks, axis=1), jnp.concatenate(tables, axis=1))
        out_ref[span, 2 * width + 128 :] = codes.astype(BF)
        store(a).start()
    for a in range(arrows):
        store(a).wait()


def prep_kernel(
    arrows, block_rows, width, pos_ref, feat_ref, w_ref, key_ref, pre_ref, first_ref, up_ref
):
    pre_ref[0] = mm(feat_ref[...], w_ref[:width, :]).astype(pre_ref.dtype)
    @pl.when(pl.program_id(0) > 0)
    def _():
        up_ref[0] = w_ref[width:, :]

    @pl.when(pl.program_id(0) == 0)
    def _():
        first_ref[...] = w_ref[width:, :]
        nodes = feat_ref.shape[0]
        n0 = lax.broadcasted_iota(jnp.int32, (nodes, nodes), 0)
        n1 = lax.broadcasted_iota(jnp.int32, (nodes, nodes), 1)
        before = onehot(n1 < n0)
        slot = lax.broadcasted_iota(jnp.int32, (nodes, 256), 1)
        lane = lax.broadcasted_iota(jnp.int32, (nodes, 128), 1)
        keys = jnp.zeros((nodes, 128), F32)
        for a in range(arrows):
            block = pos_ref[:, a : a + 1] // block_rows
            member = block == slot // 8
            rank = jnp.where(member & (slot % 8 == 0), mm(before, onehot(member)), 0.0)
            key = jnp.sum(rank, axis=1, keepdims=True) + (block * 16).astype(F32)
            keys = jnp.where(lane == a, key, keys)
        key_ref[...] = keys.T[0:8, :]


STEP = 256
WIDE = 512


def keep_of(mask_ref, row, edge):
    return jnp.broadcast_to(mask_ref[row : row + 1, :], (edge, mask_ref.shape[1])).astype(BF)


def take(places):
    ids = lax.broadcasted_iota(jnp.int32, (places.shape[0], 1024), 1).astype(F32)
    return onehot(places == ids)


def head_kernel(width, got_ref, known_ref, e0_ref, e1_ref, p_ref, s_ref, f_ref):
    slots = got_ref.shape[0]
    four = slots // 4
    two = slots // 8
    group = four + two
    codes = got_ref[:, 2 * width + 128 :].astype(F32)
    p_ref[...] = (codes - 1.0) * 32.0 + pltpu.roll(codes, 127, 1)
    f_ref[...] = got_ref[:, 2 * width : 2 * width + 128].astype(F32)
    for t in range(width // 128):
        at = width + t * 128
        s_ref[t] = got_ref[:, at : at + 128].astype(F32)
    row = lax.broadcasted_iota(jnp.int32, (8, width), 0)
    for h, ref in enumerate((e0_ref, e1_ref)):
        base = h * (slots // 2)
        at = h * group
        some = p_ref[pl.ds(base + 1, four, stride=2), :][:, 2:3]
        known_ref[at : at + four, :] = jnp.broadcast_to(some, (four, 128))
        some = p_ref[pl.ds(base, two, stride=4), :][:, 4:5]
        known_ref[at + four : at + group, :] = jnp.broadcast_to(some, (two, 128))
        for t in range(width // 128):
            span = slice(t * 128, (t + 1) * 128)
            ref[0:four, span] = s_ref[t, pl.ds(base + 1, four, stride=2), :].astype(BF)
            ref[four:group, span] = f_ref[pl.ds(base + t, two, stride=4), :].astype(BF)
        place = known_ref[at : at + group, :].T[0:1, :]
        place = jnp.concatenate([place, jnp.zeros((1, width - group), F32)], axis=1)
        high = jnp.floor(place * (1.0 / 32.0)) + 1.0
        low = place - (high - 1.0) * 32.0
        ref[group:, :] = jnp.where(row == 0, high, jnp.where(row == 1, low, 0.0)).astype(BF)


def arm_kernel(
    width, got_ref, known_ref, mask_ref, row_hbm,
    x_ref, t_ref, p_ref, s0_ref, s1_ref,
    w_ref, pt_ref, s_ref, gm_ref, w_sem,
):
    slots = got_ref.shape[0]
    size = x_ref.shape[0]
    half = slots // 2
    lanes = range(0, width, 128)
    load = pltpu.make_async_copy(row_hbm, w_ref, w_sem)
    load.start()
    codes = got_ref[:, 2 * width + 128 :].astype(F32)
    place = (codes - 1.0) * 32.0 + pltpu.roll(codes, 127, 1)
    p_ref[0:slots, :] = place
    pt_ref[:, 0:slots] = place.T[0:8, :]
    part = p_ref[pl.ds(0, half, stride=2), :]
    p_ref[slots:, :] = part
    pt_ref[:, slots:] = part.T[0:8, :]
    for j in lanes:
        s_ref[j // 128] = got_ref[:, width + j : width + j + 128].astype(F32)
        gm_ref[:, j : j + 128] = s_ref[j // 128, pl.ds(0, half, stride=2), :].astype(BF)

    def unpack(c, carry):
        def put(row, start, count):
            ids = (lax.broadcasted_iota(jnp.int32, (WIDE, count), 0) + c * WIDE).astype(F32)
            return onehot(pt_ref[row : row + 1, start : start + count] == ids)

        span = pl.ds(pl.multiple_of(c * WIDE, WIDE), WIDE)
        x_ref[span, :] = (
            mm(put(0, 0, slots), got_ref[:, 0:width]) + mm(put(2, slots, half), gm_ref[...])
        ).astype(BF)
        return carry

    lax.fori_loop(0, size // WIDE, unpack, 0)
    load.wait()
    tiles = mask_ref.shape[0] // 3
    edge = size // tiles
    for c in range(0, tiles, 2):
        span = slice(c * edge, (c + 2) * edge)
        keep = [keep_of(mask_ref, 2 * tiles + c + i, edge) for i in range(2)]
        kept = w_ref[span, :] * jnp.concatenate(keep, axis=0)
        t_ref[span, :] = mm(kept, x_ref[...]).astype(BF)
    group = s0_ref.shape[0]
    for d, ref in enumerate((s0_ref, s1_ref)):
        ref[...] = mm(take(known_ref[d * group : (d + 1) * group, 0:1]), t_ref[...]).astype(BF)


def block_kernel(
    width, x_ref, t_ref, p_ref, e0_ref, e1_ref, f0_ref, f1_ref, mask_ref, diag_hbm, col_hbm,
    out_hbm, extra_ref, arm_ref,
    w_ref, x0_ref, y_ref, out_ref, g_ref, pt_ref, own_ref, w_sem, out_sem,
):
    slots = out_ref.shape[0]
    size = x_ref.shape[0]
    half = slots // 2
    loads = [
        pltpu.make_async_copy(src, w_ref.at[k], w_sem.at[k])
        for k, src in enumerate((diag_hbm, col_hbm))
    ]
    for copy in loads:
        copy.start()

    group = arm_ref.shape[0] // 2
    for i, ref in enumerate((e0_ref, e1_ref, f0_ref, f1_ref)):
        span = slice(i * group, (i + 1) * group)
        g_ref[span, :] = ref[0:group, :]
        codes = ref[group:, :].astype(F32)
        pt_ref[0:1, span] = ((codes[0:1, :] - 1.0) * 32.0 + codes[1:2, :])[:, 0:group]
    own_ref[...] = jnp.broadcast_to(pt_ref[0:1, 2 * group :], (128, 2 * group)).T

    def unpack(c, carry):
        ids = lax.broadcasted_iota(jnp.int32, (WIDE, g_ref.shape[0]), 0) + c * WIDE
        span = pl.ds(pl.multiple_of(c * WIDE, WIDE), WIDE)
        x0_ref[span, :] = mm(onehot(pt_ref[0:1, :] == ids.astype(F32)), g_ref[...]).astype(BF)
        return carry

    lax.fori_loop(0, size // WIDE, unpack, 0)
    for copy in loads:
        copy.wait()
    tiles = mask_ref.shape[0] // 3
    edge = size // tiles
    for c in range(tiles):
        span = slice(c * edge, (c + 1) * edge)
        diag = w_ref[0, span, :] * keep_of(mask_ref, c, edge)
        col = w_ref[1, span, :] * keep_of(mask_ref, tiles + c, edge)
        y_ref[span, :] = (mm(diag, x_ref[...]) + mm(col, x0_ref[...])).astype(BF)

    def store(c):
        span = pl.ds(c * STEP, STEP)
        return pltpu.make_async_copy(
            out_ref.at[span, :], out_hbm.at[span, pl.ds(0, width)], out_sem.at[c]
        )

    for c in range(slots // STEP):
        span = slice(c * STEP, (c + 1) * STEP)
        out_ref[span, :] = mm(take(p_ref[span, 0:1]), y_ref[...]).astype(BF)
        store(c).start()
    for c in range(half // STEP):
        span = slice(c * STEP, (c + 1) * STEP)
        extra_ref[span, :] = mm(
            take(p_ref[slots + c * STEP : slots + (c + 1) * STEP, 2:3]), y_ref[...]
        )
    for c in range(own_ref.shape[0] // STEP):
        span = slice(c * STEP, (c + 1) * STEP)
        arm_ref[span, :] = mm(take(own_ref[span, 0:1]), t_ref[...])
    for c in range(slots // STEP):
        store(c).wait()


def join_kernel(
    width, extra_ref, arm_ref, r0_ref, r1_ref, kept_hbm, out_hbm,
    out_ref, s_ref, e_ref, out_sem,
):
    slots = out_ref.shape[0]
    half = slots // 2
    n4 = half // 4
    n2 = half // 8

    def store(c):
        span = pl.ds(c * STEP, STEP)
        return pltpu.make_async_copy(
            out_ref.at[span, :], out_hbm.at[span, pl.ds(width, width + 128)], out_sem.at[c]
        )

    for d in range(4):
        ref = (r0_ref, r1_ref)[d // 2]
        span = slice(d * STEP, (d + 1) * STEP)
        base = d // 2 * ref.shape[0]
        at = d % 2 * n4
        four = arm_ref[base + at : base + at + n4, :] + ref[at : at + n4, :].astype(F32)
        at = 2 * n4 + d % 2 * n2
        two = arm_ref[base + at : base + at + n2, :] + ref[at : at + n2, :].astype(F32)
        more = extra_ref[d * n4 : (d + 1) * n4, :]
        for j in range(0, width, 128):
            t = j // 128
            s_ref[d, t, pl.ds(0, n4, stride=2), :] = more[:, j : j + 128]
            s_ref[d, t, pl.ds(1, n4, stride=2), :] = four[:, j : j + 128]
            e_ref[d, pl.ds(t, n2, stride=4), :] = two[:, j : j + 128]
        for t in range(width // 128):
            out_ref[span, t * 128 : (t + 1) * 128] = s_ref[d, t].astype(BF)
        out_ref[span, width:] = e_ref[d].astype(BF)
        store(d).start()
    for d in range(4):
        store(d).wait()


def tail_kernel(
    width, arrows, reply_ref, keys_ref, first_ref, pre_hbm, up_hbm, down_hbm, out_ref,
    key_ref, pick_ref, fold_ref, flat_ref, pre_ref, up_ref, down_ref, agg_ref, acc_ref, sem,
):
    slots = reply_ref.shape[0]
    count, nodes, chunk = pre_ref.shape
    loads = []
    for c in range(count):
        span = pl.ds(c * chunk, chunk)
        loads.append(
            (
                pltpu.make_async_copy(pre_hbm.at[c], pre_ref.at[c], sem.at[1, c]),
                pltpu.make_async_copy(down_hbm.at[span, :], down_ref.at[span, :], sem.at[2, c]),
            )
        )
        if c > 0:
            up = pltpu.make_async_copy(up_hbm.at[c - 1], up_ref.at[c - 1], sem.at[0, c])
            loads[c] = (up, *loads[c])
        for copy in loads[c]:
            copy.start()
    rows = slots // arrows
    empty = jnp.zeros((120, nodes), F32)
    key_ref[...] = jnp.concatenate([keys_ref[...], empty], axis=0).T
    lane = lax.broadcasted_iota(jnp.int32, (1, rows), 1)
    blk = lane // 8
    block = blk * 16
    side = 1 - side_of(blk)
    r = lane % 8

    def hits(goal, a):
        return onehot(key_ref[:, a : a + 1] == goal.astype(F32))

    goals = (block + r, jnp.where(r % 2 == 0, block + 8 + r // 2, r - 1 + side))
    total = jnp.zeros(agg_ref.shape, F32)
    for q in range(2):
        for a in range(arrows):
            pick_ref[:, a * rows : (a + 1) * rows] = hits(goals[q], a)
        total = total + mm(pick_ref[...], reply_ref[:, q * width : (q + 1) * width])
    folded = slots // 4
    fold_ref[...] = reply_ref[:, 2 * width :].astype(F32)
    for t in range(width // 128):
        flat_ref[:, t * 128 : (t + 1) * 128] = fold_ref[pl.ds(t, folded, stride=4), :].astype(BF)
    lane = lax.broadcasted_iota(jnp.int32, (1, folded), 1)
    per = folded // arrows
    blk = lane % per // 2
    goal = 9 + lane % 2 * 2 - side_of(blk)
    key = key_ref[:, 0:1]
    for a in range(1, arrows):
        key = jnp.where(lane >= a * per, key_ref[:, a : a + 1], key)
    total = total + mm(onehot(key == goal.astype(F32)), flat_ref[...])
    agg_ref[...] = total.astype(BF)
    acc_ref[...] = jnp.zeros(acc_ref.shape, F32)
    for c in range(count):
        for copy in loads[c][:-1]:
            copy.wait()
        up = up_ref[c - 1] if c else first_ref[...]
        half = 0.5 * (pre_ref[c].astype(F32) + mm(agg_ref[...], up))
        hidden = (half * jnp.tanh(half) + half).astype(BF)
        loads[c][-1].wait()
        acc_ref[...] += mm(hidden, down_ref[c * chunk : (c + 1) * chunk, :])
    out_ref[...] = acc_ref[...].astype(BF)


CHUNK = 1024
PRE = BF


def neighbours(arrows, move):
    pairs = []
    for a in range(arrows):
        for x in range(4):
            for y in range(4):
                for z in range(2):
                    to_x = (x + move * (1 - a % 2)) % 4
                    to_y = (y + move * (a % 2)) % 4
                    pairs.append((a * 32 + x * 8 + y * 2 + z, a * 32 + to_x * 8 + to_y * 2 + z))
    return pairs


def params(limit):
    return pltpu.CompilerParams(vmem_limit_bytes=limit * MIB)


def body(
    features, positions, diag_values, column_values, row_values, tile_masks, up_weight, down_weight
):
    row_count, width = features.shape
    arrows = positions.shape[0]
    devices = arrows * lax.axis_size("blk")
    size = diag_values.shape[0]
    hidden = down_weight.shape[0]
    tiles = tile_masks.shape[1]
    rows = devices * 8
    longest = 2 * width + 256
    count = hidden // CHUNK
    dma = pltpu.SemaphoreType.DMA

    message = pl.pallas_call(
        functools.partial(pack_kernel, size, width),
        in_specs=[HB, HB],
        out_specs=HB,
        out_shape=pltpu.HBM((rows, longest), BF),
        scratch_shapes=[
            pltpu.VMEM(features.shape, BF),
            pltpu.VMEM(positions.shape, jnp.int32),
            pltpu.VMEM((rows, longest), BF),
            pltpu.VMEM((arrows, rows // arrows, 128), F32),
            dma((2,)),
            dma((arrows,)),
        ],
        compiler_params=params(24),
        name="pack",
    )(in_hbm(features), in_hbm(positions))
    got = exchange(message.reshape(devices, 8, longest)).reshape(rows, longest)

    key, pre, first, up = pl.pallas_call(
        functools.partial(prep_kernel, arrows, size, width),
        grid=(count,),
        in_specs=[
            pl.BlockSpec((row_count, arrows), lambda c: (0, 0)),
            pl.BlockSpec((row_count, width), lambda c: (0, 0)),
            pl.BlockSpec((2 * width, CHUNK), lambda c: (0, c)),
        ],
        out_specs=[
            pl.BlockSpec((8, row_count), lambda c: (0, 0)),
            pl.BlockSpec((1, row_count, CHUNK), lambda c: (c, 0, 0)),
            pl.BlockSpec((width, CHUNK), lambda c: (0, 0)),
            pl.BlockSpec((1, width, CHUNK), lambda c: (jnp.maximum(c - 1, 0), 0, 0)),
        ],
        out_shape=[
            jax.ShapeDtypeStruct((8, row_count), F32),
            pltpu.HBM((count, row_count, CHUNK), PRE),
            jax.ShapeDtypeStruct((width, CHUNK), BF),
            pltpu.HBM((count - 1, width, CHUNK), BF),
        ],
        compiler_params=params(20),
        name="prep",
    )(positions.T, in_hbm(features), in_hbm(up_weight))
    keep = jnp.repeat(tile_masks.astype(F32), size // tiles, axis=2).reshape(3 * tiles, size)

    half = rows // 2
    group = half // 2 + half // 4
    part = jax.ShapeDtypeStruct((group, width), BF)
    full = jax.ShapeDtypeStruct((size, width), BF)
    piece = jax.ShapeDtypeStruct((group + 8, width), BF)
    known, *heads = pl.pallas_call(
        functools.partial(head_kernel, width),
        in_specs=[VM],
        out_specs=[VM] * 3,
        out_shape=[jax.ShapeDtypeStruct((2 * group, 128), F32), piece, piece],
        scratch_shapes=[
            pltpu.VMEM((rows, 128), F32),
            pltpu.VMEM((width // 128, rows, 128), F32),
            pltpu.VMEM((rows, 128), F32),
        ],
        compiler_params=params(8),
        name="heads",
    )(got)
    moves = [neighbours(arrows, m) for m in (1, 3)]
    heads += [lax.ppermute(g, ("arrow", "blk"), m) for g, m in zip(heads, moves)]
    x, t, p, *given = pl.pallas_call(
        functools.partial(arm_kernel, width),
        in_specs=[VM, VM, VM, HB],
        out_specs=[VM] * 5,
        out_shape=[full, full, jax.ShapeDtypeStruct((rows + half, 128), F32), part, part],
        scratch_shapes=[
            pltpu.VMEM((size, size), BF),
            pltpu.VMEM((8, rows + half), F32),
            pltpu.VMEM((width // 128, rows, 128), F32),
            pltpu.VMEM((half, width), BF),
            dma,
        ],
        compiler_params=params(16),
        name="arms",
    )(got, known, keep, in_hbm(row_values))
    taken = [lax.ppermute(g, ("arrow", "blk"), m) for g, m in zip(given, moves)]
    reply, extra, arm = pl.pallas_call(
        functools.partial(block_kernel, width),
        in_specs=[VM] * 8 + [HB, HB],
        out_specs=[HB, VM, VM],
        out_shape=[
            pltpu.HBM((rows, 2 * width + 128), BF),
            jax.ShapeDtypeStruct((half, width), F32),
            jax.ShapeDtypeStruct((2 * group, width), F32),
        ],
        scratch_shapes=[
            pltpu.VMEM((2, size, size), BF),
            pltpu.VMEM((size, width), BF),
            pltpu.VMEM((size, width), BF),
            pltpu.VMEM((rows, width), BF),
            pltpu.VMEM((4 * group, width), BF),
            pltpu.VMEM((8, 4 * group), F32),
            pltpu.VMEM((2 * group, 128), F32),
            dma((2,)),
            dma((rows // STEP,)),
        ],
        compiler_params=params(16),
        name="blocks",
    )(x, t, p, *heads, keep, in_hbm(diag_values), in_hbm(column_values))
    reply = pl.pallas_call(
        functools.partial(join_kernel, width),
        in_specs=[VM] * 4 + [HB],
        out_specs=HB,
        out_shape=pltpu.HBM((rows, 2 * width + 128), BF),
        input_output_aliases={4: 0},
        scratch_shapes=[
            pltpu.VMEM((rows, width + 128), BF),
            pltpu.VMEM((4, width // 128, STEP, 128), F32),
            pltpu.VMEM((4, STEP, 128), F32),
            dma((4,)),
        ],
        compiler_params=params(16),
        name="join",
    )(extra, arm, *taken, reply)
    reply = exchange(reply.reshape(devices, 8, 2 * width + 128)).reshape(rows, 2 * width + 128)

    return pl.pallas_call(
        functools.partial(tail_kernel, width, arrows),
        in_specs=[VM, VM, VM, HB, HB, HB],
        out_specs=VM,
        out_shape=jax.ShapeDtypeStruct((row_count, width), BF),
        scratch_shapes=[
            pltpu.VMEM((row_count, 128), F32),
            pltpu.VMEM((row_count, rows), BF),
            pltpu.VMEM((rows, 128), F32),
            pltpu.VMEM((rows // 4, width), BF),
            pltpu.VMEM((count, row_count, CHUNK), PRE),
            pltpu.VMEM((count - 1, width, CHUNK), BF),
            pltpu.VMEM((hidden, width), BF),
            pltpu.VMEM((row_count, width), BF),
            pltpu.VMEM((row_count, width), F32),
            dma((3, count)),
        ],
        compiler_params=params(40),
        name="tail",
    )(reply, key, first, in_hbm(pre), in_hbm(up), in_hbm(down_weight))


def solution(mesh):
    in_specs = (
        P(("arrow", "blk"), None),
        P(None, ("arrow", "blk")),
        P("arrow", "blk"),
        P("arrow", "blk"),
        P("arrow", "blk"),
        P(None, "arrow", "blk"),
        P(),
        P(),
    )
    out_specs = P(("arrow", "blk"), None)
    return jax.shard_map(body, mesh=mesh, in_specs=in_specs, out_specs=out_specs, check_vma=False)
```
